256 devices in a mesh: ax: 16 (over z, core), rad: 4 (over x), pit: 4 (over y).
Axes of the slice: x: 4, y: 4, z: 8, core: 2. Of those that a mesh axis runs over, the one named last changes fastest.
Arguments:
- state: float32 [256, 49, 16, 1024], P('ax', None, 'rad', 'pit'), may hold values from -6 to 6
- flux_jac: float32 [3, 7, 7], replicated, may hold values from -2 to 2
- line_coef: float32 [16, 1024], P('rad', 'pit'), may hold values from 200 to 3000
- line_mask: int32 [256, 16, 1024], P('ax', 'rad', 'pit'), may hold values 0 or 1
Outputs:
- state_next: float32 [256, 49, 16, 1024], P('ax', None, 'rad', 'pit')
The draws below stay inside these ranges and needn't reach their ends.
All inputs are finite; a program needn't handle non-finite values. No bound on the sum of `line_mask` on one device may be relied on, other than what follows from the above.
Results may differ from the reference program's by a relative error of at most 0.0003.
Values sent between devices are 32-bit elements; how exact they have to be, the bound alone decides.
A program may use at most 64 MiB of HBM per device.

```python
import math
import jax
import jax.numpy as jnp
import numpy as np
from jax import lax

HARM = 7
VARS = 7
HV = 49
NA = 256
NR = 16
NP = 1024


def place_ends(drawn, key, least, high):
    shape = drawn.shape
    spot = [jax.random.randint(jax.random.fold_in(key, axis), (), 0, shape[axis]) for axis in range(len(shape))]
    drawn = drawn.at[tuple(spot)].set(least)
    longest = shape.index(max(shape))
    spot[longest] = (spot[longest] + 1) % shape[longest]
    return drawn.at[tuple(spot)].set(high)


def steps_of(key, shape, pieces, low, largest):
    def one(dim, parts):
        steps = jax.random.uniform(jax.random.fold_in(jax.random.fold_in(key, 6), dim), (parts,), jnp.float32, low / len(pieces), largest / len(pieces))
        return jnp.repeat(jnp.exp(steps), shape[dim] // parts).reshape((-1,) + (1,) * (len(shape) - dim - 1))

    loudness = one(*pieces[0])
    for cut in pieces[1:]:
        loudness = loudness * one(*cut)
    return loudness


def noise(own_key, extent, spread, most, pieces=(), kind=jnp.bfloat16):
    factor_of = steps_of(own_key, extent, pieces, -0.22, 0.18) if pieces else 1.0
    result = jax.random.normal(own_key, extent, jnp.float32) * spread * factor_of
    return jnp.minimum(jnp.maximum(result, -most), most).astype(kind)


def setup_inputs(seed: int = 0) -> dict:
    key_of = jax.random.split(jax.random.key(seed), 5)
    return {
        "state": noise(key_of[0], (NA, HV, NR, NP), 1.0, 6.0, ((0, 16), (2, 4), (3, 4)), jnp.float32),
        "flux_jac": noise(key_of[1], (3, VARS, VARS), VARS ** -0.5, 2.0, (), jnp.float32),
        "line_coef": jnp.clip(jnp.exp(math.log(3000.0) - 2.7080502 * jax.random.uniform(key_of[2], (NR, NP), jnp.float32) ** steps_of(key_of[2], (NR, NP), ((0, 4), (1, 4)), -0.2, 0.2)), 200.0, 3000.0),
        "line_mask": place_ends((jax.random.randint(key_of[3], (NA, NR, NP), 0, 4) < 1).astype(jnp.int32), jax.random.fold_in(key_of[3], 1), 0, 1),
    }


blade_freq = 0.6
dissipation = 0.2
courant = 1.0
section_weight = 0.5

def coupling_table():
    coupling = np.zeros((HARM, HARM), np.float32)
    for harmonic in range(1, HARM // 2 + 1):
        coupling[2 * harmonic - 1, 2 * harmonic] = -harmonic * blade_freq
        coupling[2 * harmonic, 2 * harmonic - 1] = harmonic * blade_freq
    return jnp.asarray(coupling)

def flux_of(states, matrix):
    dims_all = states.shape
    by_harmonic = states.reshape(dims_all[0], HARM, VARS, dims_all[2], dims_all[3])
    speeds = 1.0 + 0.5 * jnp.tanh(states[:, 0])
    mixed_flux = jnp.einsum('vw,nhwrp->nhvrp', matrix, by_harmonic, precision=lax.Precision.HIGHEST)
    return mixed_flux.reshape(dims_all) * speeds[:, None]

def residual_of(axial_pad, radial_pad, pitch_pad, center, flux_jac):
    flux_axial = flux_of(axial_pad, flux_jac[0])
    divergence = (flux_axial[2:] - flux_axial[:-2]) * 0.5
    flux_radial = flux_of(radial_pad, flux_jac[1])
    divergence = divergence + (flux_radial[:, :, 2:] - flux_radial[:, :, :-2]) * 0.5
    flux_pitch = flux_of(pitch_pad, flux_jac[2])
    divergence = divergence + (flux_pitch[..., 2:] - flux_pitch[..., :-2]) * 0.5
    neighbours = axial_pad[2:] + axial_pad[:-2] + radial_pad[:, :, 2:] + radial_pad[:, :, :-2]
    neighbours = neighbours + pitch_pad[..., 2:] + pitch_pad[..., :-2]
    dims_all = center.shape
    by_harmonic = center.reshape(dims_all[0], HARM, VARS, dims_all[2], dims_all[3])
    coupled = jnp.einsum('hg,ngvrp->nhvrp', coupling_table(), by_harmonic, precision=lax.Precision.HIGHEST)
    return -divergence + dissipation * (neighbours - 6.0 * center) + coupled.reshape(dims_all)

def step_rhs(center, resid, coef, flux_jac):
    limit = jnp.sum(lax.optimization_barrier(jnp.max(lax.optimization_barrier(jnp.sum(jnp.abs(flux_jac), axis=2)), axis=1)))
    speeds = 1.0 + 0.5 * jnp.tanh(center[:, 0])
    radius = speeds * limit + 6.0 * dissipation + HARM // 2 * blade_freq
    factor = section_weight * courant * jnp.sqrt(1.0 + 4.0 * coef) / radius
    return factor[:, None] * resid

def reference(state, flux_jac, line_coef, line_mask):
    coef = line_coef[None] * (1.0 + line_mask.astype(jnp.float32))
    axial_pad = jnp.pad(state, ((1, 1), (0, 0), (0, 0), (0, 0)))
    radial_pad = jnp.pad(state, ((0, 0), (0, 0), (1, 1), (0, 0)))
    pitch_pad = jnp.concatenate([state[..., -1:], state, state[..., :1]], axis=3)
    resid = residual_of(axial_pad, radial_pad, pitch_pad, state, flux_jac)
    rhs = step_rhs(state, resid, coef, flux_jac)
    position = jnp.arange(NA).astype(jnp.int32)[:, None, None]
    lower = jnp.where(position > 0, -coef, 0.0)
    upper = jnp.where(position < NA - 1, -coef, 0.0)
    diagonal = 1.0 + 2.0 * coef

    def forward(carry, item):
        pivot, partial_value = carry
        low, upp, dia, right = item
        denom = dia - low * pivot
        pivot_new = upp / denom
        gain = -low / denom
        partial_new = gain[None] * partial_value + right / denom[None]
        return ((pivot_new, partial_new), (pivot_new, partial_new))
    start = (jnp.zeros((NR, NP), jnp.float32), jnp.zeros((HV, NR, NP), jnp.float32))
    unused, (pivots, partials) = lax.scan(forward, start, (lower, upper, diagonal, rhs))

    def backward(after, item):
        pivot, partial_value = item
        value = partial_value - pivot[None] * after
        return (value, value)
    unused_end, smoothed = lax.scan(backward, jnp.zeros((HV, NR, NP), jnp.float32), (pivots, partials), reverse=True)
    return state + smoothed
```

```python
import functools

import jax
import jax.numpy as jnp
from jax import lax
from jax.experimental import pallas as pl
from jax.experimental.pallas import tpu as pltpu
from jax.sharding import PartitionSpec as P

HARM = 7
VARS = 7
HV = HARM * VARS
ROWS = 16
HALF = 25
CHUNKS = 5
PIECE = HALF // CHUNKS
MESH = pl.DeviceIdType.MESH

blade_freq = 0.6
dissipation = 0.2
courant = 1.0
section_weight = 0.5

F32 = jnp.float32
TILE = (8, 128)


def remote(src, dst, send, recv, **place):
    return pltpu.make_async_remote_copy(
        src_ref=src, dst_ref=dst, send_sem=send, recv_sem=recv, device_id=place, device_id_type=MESH
    )


def roll(x, shift, axis):
    shift = shift % x.shape[axis]
    return pltpu.roll(x, shift, axis) if shift else x


def kernel(
    sizes,
    state_hbm,
    jac,
    line,
    mask,
    out_hbm,
    st,
    bb,
    rs,
    rr,
    ps,
    pr,
    pe,
    fs,
    fr,
    am,
    dlt,
    qq,
    ww,
    zz,
    fac,
    spd,
    spk,
    ends,
    part_ends,
    x1s,
    x1r,
    bch,
    cin,
    cout,
    x2s,
    pp,
    in_sem,
    out_sem,
    a_send,
    a_recv,
    r_send,
    r_recv,
    p_send,
    p_recv,
    f_send,
    f_recv,
    e_send,
    e_recv,
    x_send,
    x_recv,
    c_send,
    c_recv,
):
    nax, nrad, npit = sizes
    chips = nax // 2
    ax = lax.axis_index("ax")
    rad = lax.axis_index("rad")
    pit = lax.axis_index("pit")
    core = lax.rem(ax, 2)
    chip = lax.div(ax, 2)
    partner = ax + 1 - 2 * core
    pit_next = lax.rem(pit + 1, npit)
    pit_prev = lax.rem(pit + npit - 1, npit)
    zero = jnp.zeros(TILE, F32)
    one = jnp.ones(TILE, F32)

    load = pltpu.make_async_copy(state_hbm, st.at[pl.ds(1, ROWS)], in_sem)
    load.start()

    barrier = pltpu.get_barrier_semaphore()

    def greet(step, carry):
        pl.semaphore_signal(
            barrier, inc=1, device_id={"ax": lax.rem(ax + step, nax)}, device_id_type=MESH
        )
        return carry

    lax.fori_loop(1, nax, greet, 0)
    pl.semaphore_signal(barrier, inc=1, device_id={"pit": pit_next}, device_id_type=MESH)
    pl.semaphore_signal(barrier, inc=1, device_id={"pit": pit_prev}, device_id_type=MESH)

    @pl.when(rad > 0)
    def _():
        pl.semaphore_signal(barrier, inc=1, device_id={"rad": rad - 1}, device_id_type=MESH)

    @pl.when(rad < nrad - 1)
    def _():
        pl.semaphore_signal(barrier, inc=1, device_id={"rad": rad + 1}, device_id_type=MESH)

    for d in range(3):
        for v in range(VARS):
            for w in range(VARS):
                am[d * 49 + v * 7 + w] = jnp.full(TILE, jac[d, v, w], F32)
    limit = zero
    for d in range(3):
        largest = zero
        for v in range(VARS):
            total = zero
            for w in range(VARS):
                total = total + jnp.abs(am[d * 49 + v * 7 + w])
            largest = jnp.maximum(largest, total)
        limit = limit + largest

    base = line[...]

    def coef_of(i):
        return base * (1.0 + mask[i].astype(F32))

    a, b, c, d_, c_prev, d_prev = one, zero, zero, one, zero, one
    for i in range(ROWS):
        inv = 1.0 / coef_of(i)
        dlt[i] = inv
        c_prev, d_prev = c, d_
        a = a + inv * c
        b = b + inv * d_
        c = a + c
        d_ = b + d_
    fs[0] = a
    fs[1] = b
    fs[2] = c_prev
    fr[ax, 0] = a
    fr[ax, 1] = b
    fr[ax, 2] = c_prev

    for side, edge in ((0, 0), (1, nrad - 1)):

        @pl.when(rad == edge)
        def _():
            def clear(h, carry):
                for g in range(4):
                    for v in range(VARS):
                        rr[side, h, g, v] = zero
                return carry

            lax.fori_loop(0, HARM, clear, 0)

    @pl.when(ax == 0)
    def _():
        def clear(c, carry):
            st[0, c] = zero
            return carry

        lax.fori_loop(0, HV, clear, 0)

    @pl.when(ax == nax - 1)
    def _():
        def clear(c, carry):
            st[ROWS + 1, c] = zero
            return carry

        lax.fori_loop(0, HV, clear, 0)

    @pl.when(chip == 0)
    def _():
        for k in range(HALF):
            cin[0, k] = zero

    @pl.when(chip == chips - 1)
    def _():
        for k in range(HALF):
            cin[1, k] = zero

    for t in range(2):
        x1s[t, HV] = zero

    radial_peers = jnp.minimum(rad, 1) + jnp.minimum(nrad - 1 - rad, 1)
    pl.semaphore_wait(barrier, nax - 1 + 2 + radial_peers)
    load.wait()

    def axial_up(peer):
        return remote(st.at[ROWS], st.at[0], a_send.at[0], a_recv.at[0], ax=peer)

    def axial_down(peer):
        return remote(st.at[1], st.at[ROWS + 1], a_send.at[1], a_recv.at[1], ax=peer)

    sub = lax.broadcasted_iota(jnp.int32, TILE, 0)
    lane = lax.broadcasted_iota(jnp.int32, TILE, 1)
    row = lax.rem(sub, 4)
    is_row = [row == j for j in range(4)]

    def packed(g, c):
        rows = [st[1 + 4 * g + j, c] for j in range(4)]
        up = rows[3]
        down = rows[0]
        for j in range(3):
            up = jnp.where(is_row[j], roll(rows[j], j - 3, 0), up)
        for j in range(1, 4):
            down = jnp.where(is_row[j], roll(rows[j], j, 0), down)
        return up, down

    def speed_of(x):
        return 1.0 + 0.5 * jnp.tanh(x)

    for g in range(4):
        up, down = packed(g, 0)
        spk[0, g] = speed_of(up)
        spk[1, g] = speed_of(down)

    def radial_up(h, peer):
        return remote(rs.at[0, h], rr.at[0, h], r_send.at[0, h], r_recv.at[0, h], rad=peer)

    def radial_down(h, peer):
        return remote(rs.at[1, h], rr.at[1, h], r_send.at[1, h], r_recv.at[1, h], rad=peer)

    def radial(h, carry):
        def group(g, carry):
            su, sd = spk[0, g], spk[1, g]
            ups, downs, wups, wdowns = [], [], [], []
            for v in range(VARS):
                up, down = packed(g, h * VARS + v)
                ups.append(up)
                downs.append(down)
                wups.append(su * up)
                wdowns.append(sd * down)
            for v in range(VARS):
                tu = -2.0 * dissipation * ups[v]
                td = -2.0 * dissipation * downs[v]
                for w in range(VARS):
                    m = am[49 + v * 7 + w]
                    tu = tu - m * wups[w]
                    td = td + m * wdowns[w]
                rs[0, h, g, v] = tu
                rs[1, h, g, v] = td
            return carry

        lax.fori_loop(0, 4, group, 0)

        @pl.when(rad < nrad - 1)
        def _():
            radial_up(h, rad + 1).start()

        @pl.when(rad > 0)
        def _():
            radial_down(h, rad - 1).start()

        return carry

    lax.fori_loop(0, HARM, radial, 0)

    @pl.when(ax < nax - 1)
    def _():
        axial_up(ax + 1).start()

    @pl.when(ax > 0)
    def _():
        axial_down(ax - 1).start()

    def factor(step):
        return remote(
            fs, fr.at[ax], f_send.at[step], f_recv.at[ax], ax=lax.rem(ax + step, nax)
        )

    def send_factor(step, carry):
        factor(step).start()
        return carry

    lax.fori_loop(1, nax, send_factor, 0)

    pair = lax.div(lane, 2)

    def pack(i, carry):
        got = zero
        for c in range(HV):
            got = jnp.where(pair == c, roll(st[1 + i, c], 2 * c + 1, 1), got)
        ps[i] = got
        return carry

    lax.fori_loop(0, ROWS, pack, 0)
    pitch_next = remote(ps, pr.at[0], p_send.at[0], p_recv.at[0], pit=pit_next)
    pitch_prev = remote(ps, pr.at[1], p_send.at[1], p_recv.at[1], pit=pit_prev)
    pitch_next.start()
    pitch_prev.start()

    def tables(i, carry):
        s = speed_of(st[1 + i, 0])
        spd[1 + i] = s
        coef = coef_of(i)
        radius = s * limit + (6.0 * dissipation + HARM // 2 * blade_freq)
        fac[i] = (-0.5 * section_weight * courant) * jnp.sqrt(1.0 + 4.0 * coef) / (coef * radius)
        return carry

    lax.fori_loop(0, ROWS, tables, 0)

    pitch_next.wait_recv()
    pitch_prev.wait_recv()
    top = sub >= 4
    even = lax.rem(lane, 2) == 0

    def merge(i, carry):
        own = ps[i]
        before = jnp.where(top, pr[0, i], own)
        after = jnp.where(top, own, pr[1, i])
        both = jnp.where(even, roll(after, -1, 1), roll(before, 1, 1))
        pe[i] = roll(both, 4, 0)
        return carry

    lax.fori_loop(0, ROWS, merge, 0)

    @pl.when(ax > 0)
    def _():
        axial_up(ax - 1).wait_recv()

    @pl.when(ax < nax - 1)
    def _():
        axial_down(ax + 1).wait_recv()

    spd[0] = speed_of(st[0, 0])
    spd[ROWS + 1] = speed_of(st[ROWS + 1, 0])

    first_lane = lane == 0
    last_lane = lane == 127
    inner_low = row > 0
    inner_high = row < 3

    def sides(i, carry):
        pitched = pe[i]
        sa, sc, sb = spd[i], spd[1 + i], spd[2 + i]
        su = roll(sc, 1, 0)
        sd = roll(sc, -1, 0)
        scale = fac[i]
        sl = sr = None
        middle = []
        accs = []
        for h in range(HARM):
            d0, d1, d2, acc = [], [], [], []
            for v in range(VARS):
                c = h * VARS + v
                here, back, ahead = st[1 + i, c], st[i, c], st[2 + i, c]
                e = roll(pitched, -(2 * c + 1), 1)
                left = jnp.where(first_lane, e, roll(here, 1, 1))
                right = jnp.where(last_lane, e, roll(here, -1, 1))
                if c == 0:
                    sl, sr = speed_of(left), speed_of(right)
                under = jnp.where(inner_low, roll(here, 1, 0), 0.0)
                over = jnp.where(inner_high, roll(here, -1, 0), 0.0)
                d0.append(sb * ahead - sa * back)
                d1.append(sd * over - su * under)
                d2.append(sr * right - sl * left)
                around = ((back + ahead) + (left + right)) + (under + over)
                acc.append(12.0 * dissipation * here - 2.0 * dissipation * around)
                if h:
                    k = (h + 1) // 2
                    twin = st[1 + i, c + VARS if h % 2 else c - VARS]
                    sign = 2.0 * k * blade_freq if h % 2 else -2.0 * k * blade_freq
                    acc[v] = acc[v] + sign * twin
            for v in range(VARS):
                t = acc[v]
                for w in range(VARS):
                    t = t + am[v * 7 + w] * d0[w]
                    t = t + am[49 + v * 7 + w] * d1[w]
                    t = t + am[98 + v * 7 + w] * d2[w]
                bb[i, h * VARS + v] = scale * t
        return carry

    lax.fori_loop(0, ROWS, sides, 0)

    def arrive(step, carry):
        source = lax.rem(ax + nax - step, nax)
        remote(fs, fr.at[source], f_send.at[step], f_recv.at[source], ax=source).wait_recv()
        return carry

    lax.fori_loop(1, nax, arrive, 0)

    def entries(j):
        a, b, c_prev = fr[j, 0], fr[j, 1], fr[j, 2]
        return a, b, c_prev, (1.0 + b * c_prev) / a

    def ahead_of(j, carry):
        n, m = carry
        a, b, c_prev, d_prev = entries(j)
        return a * n + b * m, (a + c_prev) * n + (b + d_prev) * m

    n, m = lax.fori_loop(0, ax, ahead_of, (one, one))
    e_in = n / m

    def behind(t, carry):
        n, m = carry
        a, b, c_prev, d_prev = entries(nax - 1 - t)
        return d_prev * n + b * m, (c_prev + d_prev) * n + (a + b) * m

    n, m = lax.fori_loop(0, nax - 1 - ax, behind, (one, one))
    f_in = n / m

    e = e_in
    run = one
    for i in range(ROWS):
        t = dlt[i] + e
        q = 1.0 / (1.0 + t)
        e = t * q
        run = run * q
        qq[i] = q
        ww[i] = run
    f = f_in
    for i in reversed(range(ROWS)):
        t = dlt[i] + f
        s = 1.0 / (1.0 + t)
        f = t * s
        zz[i] = s
    back_run = one
    for i in range(ROWS):
        back_run = back_run * zz[i]
        zz[i] = back_run
    ends[0] = run
    ends[1] = back_run
    ends[2] = 1.0 - f_in
    ends[3] = e + f_in * qq[ROWS - 1]
    send_ends = remote(ends.at[pl.ds(0, 2)], part_ends, e_send, e_recv, ax=partner)
    send_ends.start()

    edge_low = is_row[0]
    edge_high = is_row[3]

    def eliminate(h, carry):
        @pl.when(rad > 0)
        def _():
            radial_up(h, rad - 1).wait_recv()

        @pl.when(rad < nrad - 1)
        def _():
            radial_down(h, rad + 1).wait_recv()

        def group(g, carry):
            carried, sums = list(carry[0]), list(carry[1])
            for j in range(4):
                i = 4 * g + j
                scale, q, z = fac[i], qq[i], zz[i]
                for v in range(VARS):
                    low = roll(rr[0, h, g, v], -j, 0)
                    high = roll(rr[1, h, g, v], 3 - j, 0)
                    extra = jnp.where(edge_low, low, jnp.where(edge_high, high, 0.0))
                    right = bb[i, h * VARS + v] + scale * extra
                    carried[v] = q * (right + carried[v])
                    sums[v] = sums[v] + z * right
                    bb[i, h * VARS + v] = carried[v]
            return tuple(carried), tuple(sums)

        zeros = (zero,) * VARS
        carried, sums = lax.fori_loop(0, 4, group, (zeros, zeros))
        for v in range(VARS):
            x1s[0, h * VARS + v] = carried[v]
            x1s[1, h * VARS + v] = sums[v]
        return carry

    lax.fori_loop(0, HARM, eliminate, 0)

    mine = core * HALF
    theirs = HALF - mine
    swap = remote(
        x1s.at[:, pl.ds(theirs, HALF)], x1r, x_send.at[0], x_recv.at[0], ax=partner
    )
    swap.start()
    send_ends.wait_recv()
    lower = core == 0
    alpha0 = jnp.where(lower, ends[0], part_ends[0])
    alpha1 = jnp.where(lower, part_ends[0], ends[0])
    gamma0 = jnp.where(lower, ends[1], part_ends[1])
    gamma1 = jnp.where(lower, part_ends[1], ends[1])
    through = (alpha0 * alpha1, gamma0 * gamma1)
    swap.wait_recv()

    def pair_values(t, k):
        own, other = x1s[t, mine + k], x1r[t, k]
        return jnp.where(lower, own, other), jnp.where(lower, other, own)

    for k in range(HALF):
        b0, b1 = pair_values(0, k)
        bch[0, k] = alpha1 * b0 + b1
        g0, g1 = pair_values(1, k)
        bch[1, k] = gamma0 * g1 + g0

    second_half = lax.div(2 * chip, chips)

    def chain_copy(t, k, peer):
        return remote(
            cout.at[t, pl.ds(k * PIECE, PIECE)],
            cin.at[t, pl.ds(k * PIECE, PIECE)],
            c_send.at[t, k],
            c_recv.at[t, k],
            ax=peer,
        )

    def sends(t):
        to = chip + 1 - 2 * t
        return (to >= 0) & (to < chips)

    def receives(t):
        source = chip - 1 + 2 * t
        return (source >= 0) & (source < chips)

    def direction(turn, carry):
        t = lax.rem(second_half + turn, 2)
        factor_of = jnp.where(t == 0, through[0], through[1])

        def piece(k, carry):
            @pl.when(receives(t))
            def _():
                chain_copy(t, k, ax - 2 + 4 * t).wait_recv()

            @pl.when(sends(t))
            def _():
                for m in range(PIECE):
                    at = k * PIECE + m
                    cout[t, at] = factor_of * cin[t, at] + bch[t, at]
                chain_copy(t, k, ax + 2 - 4 * t).start()

            return carry

        lax.fori_loop(0, CHUNKS, piece, 0)
        return carry

    lax.fori_loop(0, 2, direction, 0)

    for k in range(HALF):
        p, r = cin[0, k], cin[1, k]
        b0, b1 = pair_values(0, k)
        g0, g1 = pair_values(1, k)
        p1 = alpha0 * p + b0
        r0 = gamma1 * r + g1
        pp[0, mine + k] = jnp.where(lower, p, p1)
        pp[1, mine + k] = jnp.where(lower, r0, r)
        x2s[0, k] = jnp.where(lower, p1, p)
        x2s[1, k] = jnp.where(lower, r, r0)
    back = remote(
        x2s, pp.at[:, pl.ds(mine, HALF)], x_send.at[1], x_recv.at[1], ax=partner
    )
    back.start()
    back_in = remote(
        x2s, pp.at[:, pl.ds(theirs, HALF)], x_send.at[1], x_recv.at[1], ax=partner
    )
    back_in.wait_recv()

    def finish_copy(h):
        part = pl.ds(h * VARS, VARS)
        return pltpu.make_async_copy(bb.at[:, part], out_hbm.at[:, part], out_sem.at[h])

    def finish(h, carry):
        entering, after = [], []
        for v in range(VARS):
            c = h * VARS + v
            p = pp[0, c]
            whole = ends[0] * p + x1s[0, c]
            entering.append(p)
            after.append((pp[1, c] + ends[2] * whole) / ends[3])

        def back_row(t, after):
            i = ROWS - 1 - t
            q, w = qq[i], ww[i]
            following = []
            for v in range(VARS):
                c = h * VARS + v
                x = (bb[i, c] + w * entering[v]) + q * after[v]
                following.append(x)
                bb[i, c] = st[1 + i, c] + x
            return tuple(following)

        lax.fori_loop(0, ROWS, back_row, tuple(after))
        finish_copy(h).start()
        return carry

    lax.fori_loop(0, HARM, finish, 0)

    @pl.when(ax < nax - 1)
    def _():
        axial_up(ax + 1).wait_send()

    @pl.when(ax > 0)
    def _():
        axial_down(ax - 1).wait_send()

    def sent(step, carry):
        factor(step).wait_send()
        return carry

    lax.fori_loop(1, nax, sent, 0)
    pitch_next.wait_send()
    pitch_prev.wait_send()
    send_ends.wait_send()
    swap.wait_send()
    back.wait_send()

    def sent_radial(h, carry):
        @pl.when(rad < nrad - 1)
        def _():
            radial_up(h, rad + 1).wait_send()

        @pl.when(rad > 0)
        def _():
            radial_down(h, rad - 1).wait_send()

        return carry

    lax.fori_loop(0, HARM, sent_radial, 0)

    for t in range(2):

        @pl.when(sends(t))
        def _():
            def sent_piece(k, carry):
                chain_copy(t, k, ax + 2 - 4 * t).wait_send()
                return carry

            lax.fori_loop(0, CHUNKS, sent_piece, 0)

    def written(h, carry):
        finish_copy(h).wait()
        return carry

    lax.fori_loop(0, HARM, written, 0)


def solution(mesh):
    sizes = (mesh.shape["ax"], mesh.shape["rad"], mesh.shape["pit"])
    nax = sizes[0]

    def to_tiles(x):
        lead = x.shape[:-2]
        x = x.reshape(lead + (4, 2, 128))
        n = len(lead)
        x = x.transpose(tuple(range(n)) + (n + 1, n, n + 2))
        return x.reshape(lead + TILE)

    def from_tiles(x):
        lead = x.shape[:-2]
        x = x.reshape(lead + (2, 4, 128))
        n = len(lead)
        x = x.transpose(tuple(range(n)) + (n + 1, n, n + 2))
        return x.reshape(lead + (4, 256))

    def vmem(*lead):
        return pltpu.VMEM(lead + TILE, F32)

    dma = pltpu.SemaphoreType.DMA

    def on_device(state, flux_jac, line_coef, line_mask):
        out = pl.pallas_call(
            functools.partial(kernel, sizes),
            out_shape=jax.ShapeDtypeStruct((ROWS, HV) + TILE, F32),
            in_specs=[
                pl.BlockSpec(memory_space=pl.ANY),
                pl.BlockSpec(memory_space=pltpu.SMEM),
                pl.BlockSpec(memory_space=pltpu.VMEM),
                pl.BlockSpec(memory_space=pltpu.VMEM),
            ],
            out_specs=pl.BlockSpec(memory_space=pl.ANY),
            scratch_shapes=[
                vmem(ROWS + 2, HV),
                vmem(ROWS, HV),
                vmem(2, HARM, 4, VARS),
                vmem(2, HARM, 4, VARS),
                vmem(ROWS),
                vmem(2, ROWS),
                vmem(ROWS),
                vmem(3),
                vmem(nax, 3),
                vmem(3 * VARS * VARS),
                vmem(ROWS),
                vmem(ROWS),
                vmem(ROWS),
                vmem(ROWS),
                vmem(ROWS),
                vmem(ROWS + 2),
                vmem(2, 4),
                vmem(4),
                vmem(2),
                vmem(2, 2 * HALF),
                vmem(2, HALF),
                vmem(2, HALF),
                vmem(2, HALF),
                vmem(2, HALF),
                vmem(2, HALF),
                vmem(2, 2 * HALF),
                dma,
                dma((HARM,)),
                dma((2,)),
                dma((2,)),
                dma((2, HARM)),
                dma((2, HARM)),
                dma((2,)),
                dma((2,)),
                dma((nax,)),
                dma((nax,)),
                dma,
                dma,
                dma((2,)),
                dma((2,)),
                dma((2, CHUNKS)),
                dma((2, CHUNKS)),
            ],
            compiler_params=pltpu.CompilerParams(
                collective_id=0, has_side_effects=True, vmem_limit_bytes=40 * 1024 * 1024
            ),
        )(to_tiles(state), flux_jac, to_tiles(line_coef), to_tiles(line_mask))
        return from_tiles(out)

    return jax.shard_map(
        on_device,
        mesh=mesh,
        in_specs=(P("ax", None, "rad", "pit"), P(), P("rad", "pit"), P("ax", "rad", "pit")),
        out_specs=P("ax", None, "rad", "pit"),
        check_vma=False,
    )
```

```python
import functools

import jax
import jax.numpy as jnp
from jax import lax
from jax.experimental import pallas as pl
from jax.experimental.pallas import tpu as pltpu
from jax.sharding import PartitionSpec as P

HARM = 7
VARS = 7
HV = HARM * VARS
ROWS = 16
MESH = pl.DeviceIdType.MESH

blade_freq = 0.6
dissipation = 0.2
courant = 1.0
section_weight = 0.5

F32 = jnp.float32
TILE = (8, 128)


def remote(src, dst, send, recv, **place):
    return pltpu.make_async_remote_copy(
        src_ref=src, dst_ref=dst, send_sem=send, recv_sem=recv, device_id=place, device_id_type=MESH
    )


def roll(x, shift, axis):
    shift = shift % x.shape[axis]
    return pltpu.roll(x, shift, axis) if shift else x


def kernel(
    sizes,
    state_hbm,
    jac_hbm,
    line_hbm,
    mask_hbm,
    out_hbm,
    jac,
    line,
    mask,
    st,
    bb,
    rs,
    rr,
    ps,
    pr,
    pe,
    fs,
    fr,
    am,
    dlt,
    qq,
    ww,
    zz,
    fac,
    spd,
    spk,
    ends,
    part_ends,
    x1s,
    x1r,
    cin,
    cout,
    x2s,
    x2r,
    in_sem,
    out_sem,
    a_send,
    a_recv,
    r_send,
    r_recv,
    p_send,
    p_recv,
    f_send,
    f_recv,
    e_send,
    e_recv,
    s_send,
    s_recv,
    b_send,
    b_recv,
    c_send,
    c_recv,
):
    nax, nrad, npit = sizes
    chips = nax // 2
    ax = lax.axis_index("ax")
    rad = lax.axis_index("rad")
    pit = lax.axis_index("pit")
    core = lax.rem(ax, 2)
    chip = lax.div(ax, 2)
    partner = ax + 1 - 2 * core
    pit_next = lax.rem(pit + 1, npit)
    pit_prev = lax.rem(pit + npit - 1, npit)
    zero = jnp.zeros(TILE, F32)
    one = jnp.ones(TILE, F32)

    load = pltpu.make_async_copy(state_hbm, st.at[pl.ds(1, ROWS)], in_sem.at[0])
    load.start()
    load_jac = pltpu.make_async_copy(jac_hbm, jac, in_sem.at[1])
    load_jac.start()
    load_line = pltpu.make_async_copy(line_hbm, line, in_sem.at[2])
    load_line.start()
    load_mask = pltpu.make_async_copy(mask_hbm, mask, in_sem.at[3])
    load_mask.start()

    barrier = pltpu.get_barrier_semaphore()

    def greet(step, carry):
        pl.semaphore_signal(
            barrier, inc=1, device_id={"ax": lax.rem(ax + step, nax)}, device_id_type=MESH
        )
        return carry

    lax.fori_loop(1, nax, greet, 0)
    pl.semaphore_signal(barrier, inc=1, device_id={"pit": pit_next}, device_id_type=MESH)
    pl.semaphore_signal(barrier, inc=1, device_id={"pit": pit_prev}, device_id_type=MESH)

    @pl.when(rad > 0)
    def _():
        pl.semaphore_signal(barrier, inc=1, device_id={"rad": rad - 1}, device_id_type=MESH)

    @pl.when(rad < nrad - 1)
    def _():
        pl.semaphore_signal(barrier, inc=1, device_id={"rad": rad + 1}, device_id_type=MESH)

    load_jac.wait()
    for d in range(3):
        for v in range(VARS):
            for w in range(VARS):
                am[d * 49 + v * 7 + w] = jnp.full(TILE, jac[d, v, w], F32)
    limit = zero
    for d in range(3):
        largest = zero
        for v in range(VARS):
            total = zero
            for w in range(VARS):
                total = total + jnp.abs(am[d * 49 + v * 7 + w])
            largest = jnp.maximum(largest, total)
        limit = limit + largest

    load_line.wait()
    load_mask.wait()
    base = line[...]

    def coef_of(i):
        return base * (1.0 + mask[i].astype(F32))

    a, b, c, d_, c_prev, d_prev = one, zero, zero, one, zero, one
    for i in range(ROWS):
        inv = 1.0 / coef_of(i)
        dlt[i] = inv
        c_prev, d_prev = c, d_
        a = a + inv * c
        b = b + inv * d_
        c = a + c
        d_ = b + d_
    fs[0] = a
    fs[1] = b
    fs[2] = c_prev
    fs[3] = d_prev

    for side, edge in ((0, 0), (1, nrad - 1)):

        @pl.when(rad == edge)
        def _():
            def clear(h, carry):
                for g in range(4):
                    for v in range(VARS):
                        rr[side, h, g, v] = zero
                return carry

            lax.fori_loop(0, HARM, clear, 0)

    @pl.when(ax == 0)
    def _():
        def clear(c, carry):
            st[0, c] = zero
            return carry

        lax.fori_loop(0, HV, clear, 0)

    @pl.when(ax == nax - 1)
    def _():
        def clear(c, carry):
            st[ROWS + 1, c] = zero
            return carry

        lax.fori_loop(0, HV, clear, 0)

    far = jnp.where(core == 0, chip, chips - 1 - chip)
    passes = far < chips - 1
    gets = far > 0
    chain_to = ax + 2 - 4 * core
    chain_from = ax - 2 + 4 * core

    @pl.when(far == 0)
    def _():
        for c in range(HV):
            cin[c] = zero

    load.wait()

    def axial_up(peer):
        return remote(st.at[ROWS], st.at[0], a_send.at[0], a_recv.at[0], ax=peer)

    def axial_down(peer):
        return remote(st.at[1], st.at[ROWS + 1], a_send.at[1], a_recv.at[1], ax=peer)

    sub = lax.broadcasted_iota(jnp.int32, TILE, 0)
    lane = lax.broadcasted_iota(jnp.int32, TILE, 1)

    pair = lax.div(lane, 2)

    def pack(i, carry):
        got = zero
        for c in range(HV):
            got = jnp.where(pair == c, roll(st[1 + i, c], 2 * c + 1, 1), got)
        ps[i] = got
        return carry

    lax.fori_loop(0, ROWS, pack, 0)
    pitch_next = remote(ps, pr.at[0], p_send.at[0], p_recv.at[0], pit=pit_next)
    pitch_prev = remote(ps, pr.at[1], p_send.at[1], p_recv.at[1], pit=pit_prev)

    row = lax.rem(sub, 4)
    is_row = [row == j for j in range(4)]

    def packed(g, c):
        rows = [st[1 + 4 * g + j, c] for j in range(4)]
        up = rows[3]
        down = rows[0]
        for j in range(3):
            up = jnp.where(is_row[j], roll(rows[j], j - 3, 0), up)
        for j in range(1, 4):
            down = jnp.where(is_row[j], roll(rows[j], j, 0), down)
        return up, down

    def speed_of(x):
        return 1.0 + 0.5 * jnp.tanh(x)

    for g in range(4):
        up, down = packed(g, 0)
        spk[0, g] = speed_of(up)
        spk[1, g] = speed_of(down)

    def radial_up(h, peer):
        return remote(rs.at[0, h], rr.at[0, h], r_send.at[0, h], r_recv.at[0, h], rad=peer)

    def radial_down(h, peer):
        return remote(rs.at[1, h], rr.at[1, h], r_send.at[1, h], r_recv.at[1, h], rad=peer)

    def radial(h, carry):
        def group(g, carry):
            su, sd = spk[0, g], spk[1, g]
            ups, downs, wups, wdowns = [], [], [], []
            for v in range(VARS):
                up, down = packed(g, h * VARS + v)
                ups.append(up)
                downs.append(down)
                wups.append(su * up)
                wdowns.append(sd * down)
            for v in range(VARS):
                tu = -2.0 * dissipation * ups[v]
                td = -2.0 * dissipation * downs[v]
                for w in range(VARS):
                    m = am[49 + v * 7 + w]
                    tu = tu - m * wups[w]
                    td = td + m * wdowns[w]
                rs[0, h, g, v] = tu
                rs[1, h, g, v] = td
            return carry

        lax.fori_loop(0, 4, group, 0)

        return carry

    lax.fori_loop(0, HARM, radial, 0)

    def factor(step):
        return remote(
            fs, fr.at[ax], f_send.at[step], f_recv.at[ax], ax=lax.rem(ax + step, nax)
        )

    def tables(i, carry):
        s = speed_of(st[1 + i, 0])
        spd[1 + i] = s
        coef = coef_of(i)
        radius = s * limit + (6.0 * dissipation + HARM // 2 * blade_freq)
        fac[i] = (-0.5 * section_weight * courant) * jnp.sqrt(1.0 + 4.0 * coef) / (coef * radius)
        return carry

    lax.fori_loop(0, ROWS, tables, 0)

    radial_peers = jnp.minimum(rad, 1) + jnp.minimum(nrad - 1 - rad, 1)
    pl.semaphore_wait(barrier, nax - 1 + 2 + radial_peers)
    pitch_next.start()
    pitch_prev.start()

    @pl.when(ax < nax - 1)
    def _():
        axial_up(ax + 1).start()

    @pl.when(ax > 0)
    def _():
        axial_down(ax - 1).start()

    def send_radial(h, carry):
        @pl.when(rad < nrad - 1)
        def _():
            radial_up(h, rad + 1).start()

        @pl.when(rad > 0)
        def _():
            radial_down(h, rad - 1).start()

        return carry

    lax.fori_loop(0, HARM, send_radial, 0)

    def send_factor(step, carry):
        factor(step).start()
        return carry

    lax.fori_loop(1, nax, send_factor, 0)


    pitch_next.wait_recv()
    pitch_prev.wait_recv()
    top = sub >= 4
    even = lax.rem(lane, 2) == 0

    def merge(i, carry):
        own = ps[i]
        before = jnp.where(top, pr[0, i], own)
        after = jnp.where(top, own, pr[1, i])
        both = jnp.where(even, roll(after, -1, 1), roll(before, 1, 1))
        pe[i] = roll(both, 4, 0)
        return carry

    lax.fori_loop(0, ROWS, merge, 0)

    first_lane = lane == 0
    last_lane = lane == 127
    inner_low = row > 0
    inner_high = row < 3

    def sides(step, carry):
        @pl.when(step == ROWS - 2)
        def _():
            @pl.when(ax > 0)
            def _():
                axial_up(ax - 1).wait_recv()

            @pl.when(ax < nax - 1)
            def _():
                axial_down(ax + 1).wait_recv()

            spd[0] = speed_of(st[0, 0])
            spd[ROWS + 1] = speed_of(st[ROWS + 1, 0])

        i = lax.rem(step + 1, ROWS)
        pitched = pe[i]
        sa, sc, sb = spd[i], spd[1 + i], spd[2 + i]
        su = roll(sc, 1, 0)
        sd = roll(sc, -1, 0)
        scale = fac[i]
        sl = sr = None
        middle = []
        accs = []
        for h in range(HARM):
            d0, d1, d2, acc = [], [], [], []
            for v in range(VARS):
                c = h * VARS + v
                here, back, ahead = st[1 + i, c], st[i, c], st[2 + i, c]
                e = roll(pitched, -(2 * c + 1), 1)
                left = jnp.where(first_lane, e, roll(here, 1, 1))
                right = jnp.where(last_lane, e, roll(here, -1, 1))
                if c == 0:
                    sl, sr = speed_of(left), speed_of(right)
                under = jnp.where(inner_low, roll(here, 1, 0), 0.0)
                over = jnp.where(inner_high, roll(here, -1, 0), 0.0)
                d0.append(sb * ahead - sa * back)
                d1.append(sd * over - su * under)
                d2.append(sr * right - sl * left)
                around = ((back + ahead) + (left + right)) + (under + over)
                acc.append(12.0 * dissipation * here - 2.0 * dissipation * around)
                if h:
                    k = (h + 1) // 2
                    twin = st[1 + i, c + VARS if h % 2 else c - VARS]
                    sign = 2.0 * k * blade_freq if h % 2 else -2.0 * k * blade_freq
                    acc[v] = acc[v] + sign * twin
            for v in range(VARS):
                t = acc[v]
                for w in range(VARS):
                    t = t + am[v * 7 + w] * d0[w]
                    t = t + am[49 + v * 7 + w] * d1[w]
                    t = t + am[98 + v * 7 + w] * d2[w]
                bb[i, h * VARS + v] = scale * t
        return carry

    lax.fori_loop(0, ROWS, sides, 0)

    def arrive(step, carry):
        source = lax.rem(ax + nax - step, nax)
        remote(fs, fr.at[source], f_send.at[step], f_recv.at[source], ax=source).wait_recv()
        return carry

    lax.fori_loop(1, nax, arrive, 0)

    def entries(j):
        return fr[j, 0], fr[j, 1], fr[j, 2], fr[j, 3]

    def ahead_of(j, carry):
        n, m = carry
        a, b, c_prev, d_prev = entries(j)
        return a * n + b * m, (a + c_prev) * n + (b + d_prev) * m

    n, m = lax.fori_loop(0, ax, ahead_of, (one, one))
    e_in = n / m

    def behind(t, carry):
        n, m = carry
        a, b, c_prev, d_prev = entries(nax - 1 - t)
        return d_prev * n + b * m, (c_prev + d_prev) * n + (a + b) * m

    n, m = lax.fori_loop(0, nax - 1 - ax, behind, (one, one))
    f_in = n / m

    n, m = e_in, one
    for i in range(ROWS):
        n = n + dlt[i] * m
        after = n + m
        inv = 1.0 / after
        qq[i] = m * inv
        ww[i] = inv
        m = after
    e_out = n * inv
    n, m = f_in, one
    values = []
    for i in reversed(range(ROWS)):
        values.append((i, m))
        n = n + dlt[i] * m
        m = n + m
    inv = 1.0 / m
    for i, value in values:
        zz[i] = value * inv
    ends[0] = ww[ROWS - 1]
    ends[1] = inv
    ends[2] = 1.0 - f_in
    ends[3] = 1.0 / (e_out + f_in * qq[ROWS - 1])
    send_ends = remote(ends.at[pl.ds(0, 2)], part_ends, e_send, e_recv, ax=partner)
    send_ends.start()

    edge_low = is_row[0]
    edge_high = is_row[3]

    def eliminate(h, carry):
        @pl.when(rad > 0)
        def _():
            radial_up(h, rad - 1).wait_recv()

        @pl.when(rad < nrad - 1)
        def _():
            radial_down(h, rad + 1).wait_recv()

        def group(g, carry):
            carried, sums = list(carry[0]), list(carry[1])
            for j in range(4):
                i = 4 * g + j
                scale, q, z = fac[i], qq[i], zz[i]
                for v in range(VARS):
                    low = roll(rr[0, h, g, v], -j, 0)
                    high = roll(rr[1, h, g, v], 3 - j, 0)
                    extra = jnp.where(edge_low, low, jnp.where(edge_high, high, 0.0))
                    right = bb[i, h * VARS + v] + scale * extra
                    carried[v] = q * (right + carried[v])
                    sums[v] = sums[v] + z * right
                    bb[i, h * VARS + v] = carried[v]
            return tuple(carried), tuple(sums)

        zeros = (zero,) * VARS
        carried, sums = lax.fori_loop(0, 4, group, (zeros, zeros))
        for v in range(VARS):
            x1s[0, h * VARS + v] = carried[v]
            x1s[1, h * VARS + v] = sums[v]
        return carry

    lower = core == 0

    def piece(h):
        return pl.ds(h * VARS, VARS)

    def swap(h):
        return remote(
            x1s.at[1 - core, piece(h)], x1r.at[piece(h)], s_send.at[h], s_recv.at[h], ax=partner
        )

    def chain(h, peer):
        return remote(cout.at[piece(h)], cin.at[piece(h)], c_send.at[h], c_recv.at[h], ax=peer)

    def back(h):
        return remote(x2s.at[piece(h)], x2r.at[piece(h)], b_send.at[h], b_recv.at[h], ax=partner)

    def advance(t, carry):
        @pl.when(t < HARM)
        def _():
            eliminate(t, 0)
            swap(t).start()

        @pl.when(t == 0)
        def _():
            send_ends.wait_recv()

        h = t - far

        @pl.when((h >= 0) & (h < HARM))
        def _():
            swap(h).wait_recv()

            @pl.when(gets)
            def _():
                chain(h, chain_from).wait_recv()

            own_factor = ends[core]
            other_factor = part_ends[core]
            through = own_factor * other_factor
            for v in range(VARS):
                c = h * VARS + v
                x, own = cin[c], x1s[core, c]
                cout[c] = through * x + (other_factor * own + x1r[c])
                x2s[c] = own_factor * x + own

            @pl.when(passes)
            def _():
                chain(h, chain_to).start()

            back(h).start()

        return carry

    lax.fori_loop(0, HARM + chips - 1, advance, 0)

    def finish_copy(h):
        part = pl.ds(h * VARS, VARS)
        return pltpu.make_async_copy(bb.at[:, part], out_hbm.at[:, part], out_sem.at[h])

    def finish(h, carry):
        back(h).wait_recv()
        entering, after = [], []
        for v in range(VARS):
            c = h * VARS + v
            held, given = cin[c], x2r[c]
            p = jnp.where(lower, held, given)
            r = jnp.where(lower, given, held)
            whole = ends[0] * p + x1s[0, c]
            entering.append(p)
            after.append((r + ends[2] * whole) * ends[3])

        def back_row(t, after):
            i = ROWS - 1 - t
            q, w = qq[i], ww[i]
            following = []
            for v in range(VARS):
                c = h * VARS + v
                x = (bb[i, c] + w * entering[v]) + q * after[v]
                following.append(x)
                bb[i, c] = st[1 + i, c] + x
            return tuple(following)

        lax.fori_loop(0, ROWS, back_row, tuple(after))
        finish_copy(h).start()
        return carry

    lax.fori_loop(0, HARM, finish, 0)

    @pl.when(ax < nax - 1)
    def _():
        axial_up(ax + 1).wait_send()

    @pl.when(ax > 0)
    def _():
        axial_down(ax - 1).wait_send()

    def sent(step, carry):
        factor(step).wait_send()
        return carry

    lax.fori_loop(1, nax, sent, 0)
    pitch_next.wait_send()
    pitch_prev.wait_send()
    send_ends.wait_send()

    def sent_pieces(h, carry):
        @pl.when(rad < nrad - 1)
        def _():
            radial_up(h, rad + 1).wait_send()

        @pl.when(rad > 0)
        def _():
            radial_down(h, rad - 1).wait_send()

        @pl.when(passes)
        def _():
            chain(h, chain_to).wait_send()

        swap(h).wait_send()
        back(h).wait_send()
        return carry

    lax.fori_loop(0, HARM, sent_pieces, 0)

    def written(h, carry):
        finish_copy(h).wait()
        return carry

    lax.fori_loop(0, HARM, written, 0)


def solution(mesh):
    sizes = (mesh.shape["ax"], mesh.shape["rad"], mesh.shape["pit"])
    nax = sizes[0]

    def to_tiles(x):
        lead = x.shape[:-2]
        x = x.reshape(lead + (4, 2, 128))
        n = len(lead)
        x = x.transpose(tuple(range(n)) + (n + 1, n, n + 2))
        return x.reshape(lead + TILE)

    def from_tiles(x):
        lead = x.shape[:-2]
        x = x.reshape(lead + (2, 4, 128))
        n = len(lead)
        x = x.transpose(tuple(range(n)) + (n + 1, n, n + 2))
        return x.reshape(lead + (4, 256))

    def vmem(*lead):
        return pltpu.VMEM(lead + TILE, F32)

    dma = pltpu.SemaphoreType.DMA

    def on_device(state, flux_jac, line_coef, line_mask):
        out = pl.pallas_call(
            functools.partial(kernel, sizes),
            out_shape=jax.ShapeDtypeStruct((ROWS, HV) + TILE, F32),
            in_specs=[
                pl.BlockSpec(memory_space=pltpu.HBM),
                pl.BlockSpec(memory_space=pltpu.HBM),
                pl.BlockSpec(memory_space=pltpu.HBM),
                pl.BlockSpec(memory_space=pltpu.HBM),
            ],
            out_specs=pl.BlockSpec(memory_space=pl.ANY),
            scratch_shapes=[
                pltpu.SMEM((3, VARS, VARS), F32),
                vmem(),
                pltpu.VMEM((ROWS,) + TILE, jnp.int32),
                vmem(ROWS + 2, HV),
                vmem(ROWS, HV),
                vmem(2, HARM, 4, VARS),
                vmem(2, HARM, 4, VARS),
                vmem(ROWS),
                vmem(2, ROWS),
                vmem(ROWS),
                vmem(4),
                vmem(nax, 4),
                vmem(3 * VARS * VARS),
                vmem(ROWS),
                vmem(ROWS),
                vmem(ROWS),
                vmem(ROWS),
                vmem(ROWS),
                vmem(ROWS + 2),
                vmem(2, 4),
                vmem(4),
                vmem(2),
                vmem(2, HV),
                vmem(HV),
                vmem(HV),
                vmem(HV),
                vmem(HV),
                vmem(HV),
                dma((4,)),
                dma((HARM,)),
                dma((2,)),
                dma((2,)),
                dma((2, HARM)),
                dma((2, HARM)),
                dma((2,)),
                dma((2,)),
                dma((nax,)),
                dma((nax,)),
                dma,
                dma,
                dma((HARM,)),
                dma((HARM,)),
                dma((HARM,)),
                dma((HARM,)),
                dma((HARM,)),
                dma((HARM,)),
            ],
            compiler_params=pltpu.CompilerParams(
                collective_id=0, has_side_effects=True, vmem_limit_bytes=40 * 1024 * 1024
            ),
        )(*(pltpu.with_memory_space_constraint(x, pltpu.HBM) for x in (to_tiles(state), flux_jac, to_tiles(line_coef), to_tiles(line_mask))))
        return from_tiles(out)

    return jax.shard_map(
        on_device,
        mesh=mesh,
        in_specs=(P("ax", None, "rad", "pit"), P(), P("rad", "pit"), P("ax", "rad", "pit")),
        out_specs=P("ax", None, "rad", "pit"),
        check_vma=False,
    )
```

```python
import functools

import jax
import jax.numpy as jnp
from jax import lax
from jax.experimental import pallas as pl
from jax.experimental.pallas import tpu as pltpu
from jax.sharding import PartitionSpec as P

HARM = 7
VARS = 7
HV = HARM * VARS
ROWS = 16
MESH = pl.DeviceIdType.MESH

blade_freq = 0.6
dissipation = 0.2
courant = 1.0
section_weight = 0.5

F32 = jnp.float32
TILE = (8, 128)


def remote(src, dst, send, recv, **place):
    return pltpu.make_async_remote_copy(
        src_ref=src, dst_ref=dst, send_sem=send, recv_sem=recv, device_id=place, device_id_type=MESH
    )


def roll(x, shift, axis):
    shift = shift % x.shape[axis]
    return pltpu.roll(x, shift, axis) if shift else x


def kernel(
    sizes,
    state_hbm,
    jac_hbm,
    line_hbm,
    mask_hbm,
    out_hbm,
    jac,
    line,
    mask,
    st,
    bb,
    rs,
    rr,
    ps,
    pr,
    pe,
    fs,
    fr,
    am,
    dlt,
    qq,
    ww,
    fac,
    spd,
    spk,
    ends,
    part_ends,
    x1s,
    x1r,
    cin,
    cout,
    x2s,
    x2r,
    wl,
    wsend,
    wrecv,
    part_s,
    part_r,
    in_sem,
    out_sem,
    a_send,
    a_recv,
    r_send,
    r_recv,
    p_send,
    p_recv,
    f_send,
    f_recv,
    e_send,
    e_recv,
    s_send,
    s_recv,
    b_send,
    b_recv,
    c_send,
    c_recv,
    w_send,
    w_recv,
    q_send,
    q_recv,
):
    nax, nrad, npit = sizes
    chips = nax // 2
    ax = lax.axis_index("ax")
    rad = lax.axis_index("rad")
    pit = lax.axis_index("pit")
    core = lax.rem(ax, 2)
    chip = lax.div(ax, 2)
    partner = ax + 1 - 2 * core
    pit_next = lax.rem(pit + 1, npit)
    pit_prev = lax.rem(pit + npit - 1, npit)
    zero = jnp.zeros(TILE, F32)
    one = jnp.ones(TILE, F32)

    load = pltpu.make_async_copy(state_hbm, st.at[pl.ds(1, ROWS)], in_sem.at[0])
    load.start()
    load_jac = pltpu.make_async_copy(jac_hbm, jac, in_sem.at[1])
    load_jac.start()
    load_line = pltpu.make_async_copy(line_hbm, line, in_sem.at[2])
    load_line.start()
    load_mask = pltpu.make_async_copy(mask_hbm, mask, in_sem.at[3])
    load_mask.start()

    barrier = pltpu.get_barrier_semaphore()

    def greet(step, carry):
        pl.semaphore_signal(
            barrier, inc=1, device_id={"ax": lax.rem(ax + step, nax)}, device_id_type=MESH
        )
        return carry

    lax.fori_loop(1, nax, greet, 0)
    pl.semaphore_signal(barrier, inc=1, device_id={"pit": pit_next}, device_id_type=MESH)
    pl.semaphore_signal(barrier, inc=1, device_id={"pit": pit_prev}, device_id_type=MESH)

    @pl.when(rad > 0)
    def _():
        pl.semaphore_signal(barrier, inc=1, device_id={"rad": rad - 1}, device_id_type=MESH)

    @pl.when(rad < nrad - 1)
    def _():
        pl.semaphore_signal(barrier, inc=1, device_id={"rad": rad + 1}, device_id_type=MESH)

    load_jac.wait()
    for d in range(3):
        for v in range(VARS):
            for w in range(VARS):
                am[d * 49 + v * 7 + w] = jnp.full(TILE, jac[d, v, w], F32)
    limit = zero
    for d in range(3):
        largest = zero
        for v in range(VARS):
            total = zero
            for w in range(VARS):
                total = total + jnp.abs(am[d * 49 + v * 7 + w])
            largest = jnp.maximum(largest, total)
        limit = limit + largest

    load_line.wait()
    load_mask.wait()
    base = line[...]

    def coef_of(i):
        return base * (1.0 + mask[i].astype(F32))

    a, b, c, d_, c_prev, d_prev = one, zero, zero, one, zero, one
    heads = []
    for i in range(ROWS):
        inv = 1.0 / coef_of(i)
        dlt[i] = inv
        heads.append(c + d_)
        c_prev, d_prev = c, d_
        a = a + inv * c
        b = b + inv * d_
        c = a + c
        d_ = b + d_
    inv = 1.0 / (c + d_)
    for i in range(ROWS):
        wl[0, i] = heads[i] * inv
    e_own = (a + b) * inv
    n, m = one, one
    heads = []
    for i in reversed(range(ROWS)):
        heads.append((i, m))
        n = n + dlt[i] * m
        m = n + m
    inv = 1.0 / m
    for i, value in heads:
        wl[1, i] = value * inv
    f_own = n * inv
    fs[0] = a
    fs[1] = b
    fs[2] = c_prev
    fs[3] = d_prev

    for side, edge in ((0, 0), (1, nrad - 1)):

        @pl.when(rad == edge)
        def _():
            def clear(h, carry):
                for g in range(4):
                    for v in range(VARS):
                        rr[side, h, g, v] = zero
                    part_r[side, h, g] = zero
                return carry

            lax.fori_loop(0, HARM, clear, 0)

    @pl.when(ax == 0)
    def _():
        def clear(c, carry):
            st[0, c] = zero
            return carry

        lax.fori_loop(0, HV, clear, 0)

    @pl.when(ax == nax - 1)
    def _():
        def clear(c, carry):
            st[ROWS + 1, c] = zero
            return carry

        lax.fori_loop(0, HV, clear, 0)

    far = jnp.where(core == 0, chip, chips - 1 - chip)
    passes = far < chips - 1
    gets = far > 0
    chain_to = ax + 2 - 4 * core
    chain_from = ax - 2 + 4 * core

    @pl.when(far == 0)
    def _():
        for c in range(HV):
            cin[c] = zero

    load.wait()

    def axial_up(peer):
        return remote(st.at[ROWS], st.at[0], a_send.at[0], a_recv.at[0], ax=peer)

    def axial_down(peer):
        return remote(st.at[1], st.at[ROWS + 1], a_send.at[1], a_recv.at[1], ax=peer)

    sub = lax.broadcasted_iota(jnp.int32, TILE, 0)
    lane = lax.broadcasted_iota(jnp.int32, TILE, 1)

    pair = lax.div(lane, 2)

    def pack(i, carry):
        got = zero
        for c in range(HV):
            got = jnp.where(pair == c, roll(st[1 + i, c], 2 * c + 1, 1), got)
        ps[i] = got
        return carry

    lax.fori_loop(0, ROWS, pack, 0)
    pitch_next = remote(ps, pr.at[0], p_send.at[0], p_recv.at[0], pit=pit_next)
    pitch_prev = remote(ps, pr.at[1], p_send.at[1], p_recv.at[1], pit=pit_prev)

    row = lax.rem(sub, 4)
    is_row = [row == j for j in range(4)]

    def packed_rows(rows):
        up = rows[3]
        down = rows[0]
        for j in range(3):
            up = jnp.where(is_row[j], roll(rows[j], j - 3, 0), up)
        for j in range(1, 4):
            down = jnp.where(is_row[j], roll(rows[j], j, 0), down)
        return up, down

    def packed(g, c):
        return packed_rows([st[1 + 4 * g + j, c] for j in range(4)])

    def speed_of(x):
        return 1.0 + 0.5 * jnp.tanh(x)

    for g in range(4):
        up, down = packed(g, 0)
        spk[0, g] = speed_of(up)
        spk[1, g] = speed_of(down)

    def radial_up(h, peer):
        return remote(rs.at[0, h], rr.at[0, h], r_send.at[0, h], r_recv.at[0, h], rad=peer)

    def radial_down(h, peer):
        return remote(rs.at[1, h], rr.at[1, h], r_send.at[1, h], r_recv.at[1, h], rad=peer)

    def radial(h, carry):
        def group(g, carry):
            su, sd = spk[0, g], spk[1, g]
            ups, downs, wups, wdowns = [], [], [], []
            for v in range(VARS):
                up, down = packed(g, h * VARS + v)
                ups.append(up)
                downs.append(down)
                wups.append(su * up)
                wdowns.append(sd * down)
            for v in range(VARS):
                tu = -2.0 * dissipation * ups[v]
                td = -2.0 * dissipation * downs[v]
                for w in range(VARS):
                    m = am[49 + v * 7 + w]
                    tu = tu - m * wups[w]
                    td = td + m * wdowns[w]
                rs[0, h, g, v] = tu
                rs[1, h, g, v] = td
            return carry

        lax.fori_loop(0, 4, group, 0)

        return carry

    lax.fori_loop(0, HARM, radial, 0)

    def factor(step):
        return remote(
            fs, fr.at[ax], f_send.at[step], f_recv.at[ax], ax=lax.rem(ax + step, nax)
        )

    def tables(i, carry):
        s = speed_of(st[1 + i, 0])
        spd[1 + i] = s
        coef = coef_of(i)
        radius = s * limit + (6.0 * dissipation + HARM // 2 * blade_freq)
        fac[i] = (-0.5 * section_weight * courant) * jnp.sqrt(1.0 + 4.0 * coef) / (coef * radius)
        return carry

    lax.fori_loop(0, ROWS, tables, 0)

    for t in range(2):
        for g in range(4):
            up, down = packed_rows([fac[4 * g + j] * wl[t, 4 * g + j] for j in range(4)])
            wsend[0, t, g] = down
            wsend[1, t, g] = up

    def weights(side, peer):
        return remote(wsend.at[side], wrecv.at[side], w_send.at[side], w_recv.at[side], rad=peer)

    def partial(side, peer):
        return remote(part_s.at[side], part_r.at[side], q_send.at[side], q_recv.at[side], rad=peer)

    radial_peers = jnp.minimum(rad, 1) + jnp.minimum(nrad - 1 - rad, 1)
    pl.semaphore_wait(barrier, nax - 1 + 2 + radial_peers)
    pitch_next.start()
    pitch_prev.start()

    @pl.when(ax < nax - 1)
    def _():
        axial_up(ax + 1).start()

    @pl.when(ax > 0)
    def _():
        axial_down(ax - 1).start()

    def send_radial(h, carry):
        @pl.when(rad < nrad - 1)
        def _():
            radial_up(h, rad + 1).start()

        @pl.when(rad > 0)
        def _():
            radial_down(h, rad - 1).start()

        return carry

    @pl.when(rad > 0)
    def _():
        weights(0, rad - 1).start()

    @pl.when(rad < nrad - 1)
    def _():
        weights(1, rad + 1).start()

    lax.fori_loop(0, 2, send_radial, 0)

    def send_factor(step, carry):
        factor(step).start()
        return carry

    lax.fori_loop(1, nax, send_factor, 0)


    def weigh(side):
        def harmonic(h, carry):
            for pair_at in range(4):
                got = zero
                for m in range(4):
                    v = 2 * pair_at + m // 2
                    if v == VARS:
                        continue
                    x = zero
                    for g in range(4):
                        x = x + wrecv[side, m % 2, g] * rs[side, h, g, v]
                    turn = 1 if side else -1
                    x = x + roll(x, turn, 0)
                    x = x + roll(x, 2 * turn, 0)
                    target = 3 - m if side else m
                    got = jnp.where(is_row[target], roll(x, -turn * m, 0), got)
                part_s[side, h, pair_at] = got
            return carry

        lax.fori_loop(0, HARM, harmonic, 0)

    @pl.when(rad < nrad - 1)
    def _():
        weights(0, rad + 1).wait_recv()
        weigh(0)
        partial(0, rad + 1).start()

    @pl.when(rad > 0)
    def _():
        weights(1, rad - 1).wait_recv()
        weigh(1)
        partial(1, rad - 1).start()

    lax.fori_loop(2, HARM, send_radial, 0)

    pitch_next.wait_recv()
    pitch_prev.wait_recv()
    top = sub >= 4
    even = lax.rem(lane, 2) == 0

    def merge(i, carry):
        own = ps[i]
        before = jnp.where(top, pr[0, i], own)
        after = jnp.where(top, own, pr[1, i])
        both = jnp.where(even, roll(after, -1, 1), roll(before, 1, 1))
        pe[i] = roll(both, 4, 0)
        return carry

    lax.fori_loop(0, ROWS, merge, 0)

    first_lane = lane == 0
    last_lane = lane == 127
    inner_low = row > 0
    inner_high = row < 3

    def sides(step, carry):
        @pl.when(step == ROWS - 2)
        def _():
            @pl.when(ax > 0)
            def _():
                axial_up(ax - 1).wait_recv()

            @pl.when(ax < nax - 1)
            def _():
                axial_down(ax + 1).wait_recv()

            spd[0] = speed_of(st[0, 0])
            spd[ROWS + 1] = speed_of(st[ROWS + 1, 0])

        i = lax.rem(step + 1, ROWS)
        pitched = pe[i]
        sa, sc, sb = spd[i], spd[1 + i], spd[2 + i]
        su = roll(sc, 1, 0)
        sd = roll(sc, -1, 0)
        scale = fac[i]
        sl = sr = None
        middle = []
        accs = []
        for h in range(HARM):
            d0, d1, d2, acc = [], [], [], []
            for v in range(VARS):
                c = h * VARS + v
                here, back, ahead = st[1 + i, c], st[i, c], st[2 + i, c]
                e = roll(pitched, -(2 * c + 1), 1)
                left = jnp.where(first_lane, e, roll(here, 1, 1))
                right = jnp.where(last_lane, e, roll(here, -1, 1))
                if c == 0:
                    sl, sr = speed_of(left), speed_of(right)
                under = jnp.where(inner_low, roll(here, 1, 0), 0.0)
                over = jnp.where(inner_high, roll(here, -1, 0), 0.0)
                d0.append(sb * ahead - sa * back)
                d1.append(sd * over - su * under)
                d2.append(sr * right - sl * left)
                around = ((back + ahead) + (left + right)) + (under + over)
                acc.append(12.0 * dissipation * here - 2.0 * dissipation * around)
                if h:
                    k = (h + 1) // 2
                    twin = st[1 + i, c + VARS if h % 2 else c - VARS]
                    sign = 2.0 * k * blade_freq if h % 2 else -2.0 * k * blade_freq
                    acc[v] = acc[v] + sign * twin
            for v in range(VARS):
                t = acc[v]
                for w in range(VARS):
                    t = t + am[v * 7 + w] * d0[w]
                    t = t + am[49 + v * 7 + w] * d1[w]
                    t = t + am[98 + v * 7 + w] * d2[w]
                bb[i, h * VARS + v] = scale * t
        return carry

    lax.fori_loop(0, ROWS, sides, 0)

    def arrive(step, carry):
        source = lax.rem(ax + nax - step, nax)
        remote(fs, fr.at[source], f_send.at[step], f_recv.at[source], ax=source).wait_recv()
        return carry

    lax.fori_loop(1, nax, arrive, 0)

    def entries(j):
        return fr[j, 0], fr[j, 1], fr[j, 2], fr[j, 3]

    def ahead_of(j, carry):
        n, m = carry
        a, b, c_prev, d_prev = entries(j)
        return a * n + b * m, (a + c_prev) * n + (b + d_prev) * m

    n, m = lax.fori_loop(0, ax, ahead_of, (one, one))
    e_in = n / m

    def behind(t, carry):
        n, m = carry
        a, b, c_prev, d_prev = entries(nax - 1 - t)
        return d_prev * n + b * m, (c_prev + d_prev) * n + (a + b) * m

    n, m = lax.fori_loop(0, nax - 1 - ax, behind, (one, one))
    f_in = n / m

    n, m = e_in, one
    for i in range(ROWS):
        n = n + dlt[i] * m
        after = n + m
        inv = 1.0 / after
        qq[i] = m * inv
        ww[i] = inv
        m = after
    e_out = n * inv
    n, m = f_in, one
    for i in reversed(range(ROWS)):
        n = n + dlt[i] * m
        m = n + m
    inv = 1.0 / m
    ends[0] = ww[ROWS - 1]
    ends[1] = inv
    ends[2] = 1.0 - f_in
    ends[3] = 1.0 / (e_out + f_in * qq[ROWS - 1])
    send_ends = remote(ends.at[pl.ds(0, 2)], part_ends, e_send, e_recv, ax=partner)
    send_ends.start()

    edge_low = is_row[0]
    edge_high = is_row[3]
    lower = core == 0

    def piece(h):
        return pl.ds(h * VARS, VARS)

    def swap(h):
        return remote(
            x1s.at[1 - core, piece(h)], x1r.at[piece(h)], s_send.at[h], s_recv.at[h], ax=partner
        )

    @pl.when(rad > 0)
    def _():
        partial(0, rad - 1).wait_recv()

    @pl.when(rad < nrad - 1)
    def _():
        partial(1, rad + 1).wait_recv()

    q_in, s_in = 1.0 - e_in, 1.0 - f_in
    mix_first = wl[1, ROWS - 1] * q_in / (e_in + f_own * q_in)
    mix_last = wl[0, 0] * s_in / (f_in + e_own * s_in)

    def block_ends(h, carry):
        def group(g, sums):
            sums = list(sums)
            for j in range(4):
                i = 4 * g + j
                last, first = wl[0, i], wl[1, i]
                for v in range(VARS):
                    right = bb[i, h * VARS + v]
                    sums[2 * v] = sums[2 * v] + last * right
                    sums[2 * v + 1] = sums[2 * v + 1] + first * right
            return tuple(sums)

        sums = list(lax.fori_loop(0, 4, group, (zero,) * (2 * VARS)))
        for at in range(2 * VARS):
            m = at % 4
            low = roll(part_r[0, h, at // 4], -m, 0)
            high = roll(part_r[1, h, at // 4], m, 0)
            sums[at] = sums[at] + jnp.where(edge_low, low, jnp.where(edge_high, high, 0.0))
        for v in range(VARS):
            x1s[0, h * VARS + v] = sums[2 * v] + mix_first * sums[2 * v + 1]
            x1s[1, h * VARS + v] = sums[2 * v + 1] + mix_last * sums[2 * v]
        swap(h).start()
        return carry

    lax.fori_loop(0, HARM, block_ends, 0)

    def eliminate(h, carry):
        @pl.when(rad > 0)
        def _():
            radial_up(h, rad - 1).wait_recv()

        @pl.when(rad < nrad - 1)
        def _():
            radial_down(h, rad + 1).wait_recv()

        def group(g, carry):
            carried = list(carry)
            for j in range(4):
                i = 4 * g + j
                scale, q = fac[i], qq[i]
                for v in range(VARS):
                    low = roll(rr[0, h, g, v], -j, 0)
                    high = roll(rr[1, h, g, v], 3 - j, 0)
                    extra = jnp.where(edge_low, low, jnp.where(edge_high, high, 0.0))
                    right = bb[i, h * VARS + v] + scale * extra
                    carried[v] = q * (right + carried[v])
                    bb[i, h * VARS + v] = carried[v]
            return tuple(carried)

        lax.fori_loop(0, 4, group, (zero,) * VARS)
        return carry

    def chain(h, peer):
        return remote(cout.at[piece(h)], cin.at[piece(h)], c_send.at[h], c_recv.at[h], ax=peer)

    def back(h):
        return remote(x2s.at[piece(h)], x2r.at[piece(h)], b_send.at[h], b_recv.at[h], ax=partner)

    send_ends.wait_recv()

    def relay(h, carry):
        swap(h).wait_recv()

        @pl.when(gets)
        def _():
            chain(h, chain_from).wait_recv()

        own_factor = ends[core]
        other_factor = part_ends[core]
        through = own_factor * other_factor
        for v in range(VARS):
            c = h * VARS + v
            x, own = cin[c], x1s[core, c]
            cout[c] = through * x + (other_factor * own + x1r[c])
            x2s[c] = own_factor * x + own

        @pl.when(passes)
        def _():
            chain(h, chain_to).start()

        back(h).start()
        return carry

    relay_turn = lax.div(far, 5)

    def turn(t, carry):
        @pl.when(t == relay_turn)
        def _():
            lax.fori_loop(0, HARM, relay, 0)

        @pl.when(t == 0)
        def _():
            lax.fori_loop(0, HARM, eliminate, 0)

        return carry

    lax.fori_loop(0, 2, turn, 0)

    def finish_copy(h):
        part = pl.ds(h * VARS, VARS)
        return pltpu.make_async_copy(bb.at[:, part], out_hbm.at[:, part], out_sem.at[h])

    def finish(h, carry):
        back(h).wait_recv()
        entering, after = [], []
        for v in range(VARS):
            c = h * VARS + v
            held, given = cin[c], x2r[c]
            p = jnp.where(lower, held, given)
            r = jnp.where(lower, given, held)
            whole = ends[0] * p + x1s[0, c]
            entering.append(p)
            after.append((r + ends[2] * whole) * ends[3])

        def back_row(t, after):
            i = ROWS - 1 - t
            q, w = qq[i], ww[i]
            following = []
            for v in range(VARS):
                c = h * VARS + v
                x = (bb[i, c] + w * entering[v]) + q * after[v]
                following.append(x)
                bb[i, c] = st[1 + i, c] + x
            return tuple(following)

        lax.fori_loop(0, ROWS, back_row, tuple(after))
        finish_copy(h).start()
        return carry

    lax.fori_loop(0, HARM, finish, 0)

    @pl.when(ax < nax - 1)
    def _():
        axial_up(ax + 1).wait_send()

    @pl.when(ax > 0)
    def _():
        axial_down(ax - 1).wait_send()

    def sent(step, carry):
        factor(step).wait_send()
        return carry

    lax.fori_loop(1, nax, sent, 0)
    pitch_next.wait_send()
    pitch_prev.wait_send()
    send_ends.wait_send()

    @pl.when(rad > 0)
    def _():
        weights(0, rad - 1).wait_send()
        partial(1, rad - 1).wait_send()

    @pl.when(rad < nrad - 1)
    def _():
        weights(1, rad + 1).wait_send()
        partial(0, rad + 1).wait_send()

    def sent_pieces(h, carry):
        @pl.when(rad < nrad - 1)
        def _():
            radial_up(h, rad + 1).wait_send()

        @pl.when(rad > 0)
        def _():
            radial_down(h, rad - 1).wait_send()

        @pl.when(passes)
        def _():
            chain(h, chain_to).wait_send()

        swap(h).wait_send()
        back(h).wait_send()
        return carry

    lax.fori_loop(0, HARM, sent_pieces, 0)

    def written(h, carry):
        finish_copy(h).wait()
        return carry

    lax.fori_loop(0, HARM, written, 0)


def solution(mesh):
    sizes = (mesh.shape["ax"], mesh.shape["rad"], mesh.shape["pit"])
    nax = sizes[0]

    def to_tiles(x):
        lead = x.shape[:-2]
        x = x.reshape(lead + (4, 2, 128))
        n = len(lead)
        x = x.transpose(tuple(range(n)) + (n + 1, n, n + 2))
        return x.reshape(lead + TILE)

    def from_tiles(x):
        lead = x.shape[:-2]
        x = x.reshape(lead + (2, 4, 128))
        n = len(lead)
        x = x.transpose(tuple(range(n)) + (n + 1, n, n + 2))
        return x.reshape(lead + (4, 256))

    def vmem(*lead):
        return pltpu.VMEM(lead + TILE, F32)

    dma = pltpu.SemaphoreType.DMA

    def on_device(state, flux_jac, line_coef, line_mask):
        out = pl.pallas_call(
            functools.partial(kernel, sizes),
            out_shape=jax.ShapeDtypeStruct((ROWS, HV) + TILE, F32),
            in_specs=[
                pl.BlockSpec(memory_space=pltpu.HBM),
                pl.BlockSpec(memory_space=pltpu.HBM),
                pl.BlockSpec(memory_space=pltpu.HBM),
                pl.BlockSpec(memory_space=pltpu.HBM),
            ],
            out_specs=pl.BlockSpec(memory_space=pl.ANY),
            scratch_shapes=[
                pltpu.SMEM((3, VARS, VARS), F32),
                vmem(),
                pltpu.VMEM((ROWS,) + TILE, jnp.int32),
                vmem(ROWS + 2, HV),
                vmem(ROWS, HV),
                vmem(2, HARM, 4, VARS),
                vmem(2, HARM, 4, VARS),
                vmem(ROWS),
                vmem(2, ROWS),
                vmem(ROWS),
                vmem(4),
                vmem(nax, 4),
                vmem(3 * VARS * VARS),
                vmem(ROWS),
                vmem(ROWS),
                vmem(ROWS),
                vmem(ROWS),
                vmem(ROWS + 2),
                vmem(2, 4),
                vmem(4),
                vmem(2),
                vmem(2, HV),
                vmem(HV),
                vmem(HV),
                vmem(HV),
                vmem(HV),
                vmem(HV),
                vmem(2, ROWS),
                vmem(2, 2, 4),
                vmem(2, 2, 4),
                vmem(2, HARM, 4),
                vmem(2, HARM, 4),
                dma((4,)),
                dma((HARM,)),
                dma((2,)),
                dma((2,)),
                dma((2, HARM)),
                dma((2, HARM)),
                dma((2,)),
                dma((2,)),
                dma((nax,)),
                dma((nax,)),
                dma,
                dma,
                dma((HARM,)),
                dma((HARM,)),
                dma((HARM,)),
                dma((HARM,)),
                dma((HARM,)),
                dma((HARM,)),
                dma((2,)),
                dma((2,)),
                dma((2,)),
                dma((2,)),
            ],
            compiler_params=pltpu.CompilerParams(
                collective_id=0, has_side_effects=True, vmem_limit_bytes=40 * 1024 * 1024
            ),
        )(*(pltpu.with_memory_space_constraint(x, pltpu.HBM) for x in (to_tiles(state), flux_jac, to_tiles(line_coef), to_tiles(line_mask))))
        return from_tiles(out)

    return jax.shard_map(
        on_device,
        mesh=mesh,
        in_specs=(P("ax", None, "rad", "pit"), P(), P("rad", "pit"), P("ax", "rad", "pit")),
        out_specs=P("ax", None, "rad", "pit"),
        check_vma=False,
    )
```

```python
import functools

import jax
import jax.numpy as jnp
from jax import lax
from jax.experimental import pallas as pl
from jax.experimental.pallas import tpu as pltpu
from jax.sharding import PartitionSpec as P

HARM = 7
VARS = 7
HV = HARM * VARS
ROWS = 16
MESH = pl.DeviceIdType.MESH

blade_freq = 0.6
dissipation = 0.2
courant = 1.0
section_weight = 0.5

F32 = jnp.float32
TILE = (8, 128)


def remote(src, dst, send, recv, **place):
    return pltpu.make_async_remote_copy(
        src_ref=src, dst_ref=dst, send_sem=send, recv_sem=recv, device_id=place, device_id_type=MESH
    )


def roll(x, shift, axis):
    shift = shift % x.shape[axis]
    return pltpu.roll(x, shift, axis) if shift else x


def kernel(
    sizes,
    state_hbm,
    jac_hbm,
    line_hbm,
    mask_hbm,
    out_hbm,
    jac,
    line,
    mask,
    st,
    bb,
    rs,
    rr,
    ps,
    pr,
    pe,
    fs,
    fx,
    mo,
    mi,
    am,
    dlt,
    qq,
    ww,
    fac,
    spd,
    spk,
    ends,
    part_ends,
    x1s,
    x1r,
    cin,
    cout,
    x2s,
    x2r,
    wl,
    wsend,
    wrecv,
    part_s,
    part_r,
    in_sem,
    out_sem,
    a_send,
    a_recv,
    r_send,
    r_recv,
    p_send,
    p_recv,
    g_send,
    g_recv,
    e_send,
    e_recv,
    s_send,
    s_recv,
    b_send,
    b_recv,
    c_send,
    c_recv,
    w_send,
    w_recv,
    q_send,
    q_recv,
):
    nax, nrad, npit = sizes
    chips = nax // 2
    ax = lax.axis_index("ax")
    rad = lax.axis_index("rad")
    pit = lax.axis_index("pit")
    core = lax.rem(ax, 2)
    chip = lax.div(ax, 2)
    partner = ax + 1 - 2 * core
    pit_next = lax.rem(pit + 1, npit)
    pit_prev = lax.rem(pit + npit - 1, npit)
    zero = jnp.zeros(TILE, F32)
    one = jnp.ones(TILE, F32)

    load = pltpu.make_async_copy(state_hbm, st.at[pl.ds(1, ROWS)], in_sem.at[0])
    load.start()
    load_jac = pltpu.make_async_copy(jac_hbm, jac, in_sem.at[1])
    load_jac.start()
    load_line = pltpu.make_async_copy(line_hbm, line, in_sem.at[2])
    load_line.start()
    load_mask = pltpu.make_async_copy(mask_hbm, mask, in_sem.at[3])
    load_mask.start()

    barrier = pltpu.get_barrier_semaphore()

    for offset in (-2, -1, 1, 2):

        @pl.when((ax + offset >= 0) & (ax + offset < nax))
        def _():
            pl.semaphore_signal(
                barrier, inc=1, device_id={"ax": ax + offset}, device_id_type=MESH
            )

    pl.semaphore_signal(barrier, inc=1, device_id={"pit": pit_next}, device_id_type=MESH)
    pl.semaphore_signal(barrier, inc=1, device_id={"pit": pit_prev}, device_id_type=MESH)

    @pl.when(rad > 0)
    def _():
        pl.semaphore_signal(barrier, inc=1, device_id={"rad": rad - 1}, device_id_type=MESH)

    @pl.when(rad < nrad - 1)
    def _():
        pl.semaphore_signal(barrier, inc=1, device_id={"rad": rad + 1}, device_id_type=MESH)

    load_jac.wait()
    for d in range(3):
        for v in range(VARS):
            for w in range(VARS):
                am[d * 49 + v * 7 + w] = jnp.full(TILE, jac[d, v, w], F32)
    limit = zero
    for d in range(3):
        largest = zero
        for v in range(VARS):
            total = zero
            for w in range(VARS):
                total = total + jnp.abs(am[d * 49 + v * 7 + w])
            largest = jnp.maximum(largest, total)
        limit = limit + largest

    load_line.wait()
    load_mask.wait()
    base = line[...]

    def coef_of(i):
        return base * (1.0 + mask[i].astype(F32))

    a, b, c, d_, c_prev, d_prev = one, zero, zero, one, zero, one
    heads = []
    for i in range(ROWS):
        inv = 1.0 / coef_of(i)
        dlt[i] = inv
        heads.append(c + d_)
        c_prev, d_prev = c, d_
        a = a + inv * c
        b = b + inv * d_
        c = a + c
        d_ = b + d_
    inv = 1.0 / (c + d_)
    for i in range(ROWS):
        wl[0, i] = heads[i] * inv
    e_own = (a + b) * inv
    n, m = one, one
    heads = []
    for i in reversed(range(ROWS)):
        heads.append((i, m))
        n = n + dlt[i] * m
        m = n + m
    inv = 1.0 / m
    for i, value in heads:
        wl[1, i] = value * inv
    f_own = n * inv
    fs[0] = a
    fs[1] = b
    fs[2] = c_prev
    fs[3] = d_prev

    for side, edge in ((0, 0), (1, nrad - 1)):

        @pl.when(rad == edge)
        def _():
            def clear(h, carry):
                for g in range(4):
                    for v in range(VARS):
                        rr[side, h, g, v] = zero
                    part_r[side, h, g] = zero
                return carry

            lax.fori_loop(0, HARM, clear, 0)

    @pl.when(ax == 0)
    def _():
        def clear(c, carry):
            st[0, c] = zero
            return carry

        lax.fori_loop(0, HV, clear, 0)

    @pl.when(ax == nax - 1)
    def _():
        def clear(c, carry):
            st[ROWS + 1, c] = zero
            return carry

        lax.fori_loop(0, HV, clear, 0)

    far = jnp.where(core == 0, chip, chips - 1 - chip)
    passes = far < chips - 1
    gets = far > 0
    chain_to = ax + 2 - 4 * core
    chain_from = ax - 2 + 4 * core

    @pl.when(far == 0)
    def _():
        mi[1] = one
        for c in range(HV):
            cin[c] = zero

    load.wait()

    def axial_up(peer):
        return remote(st.at[ROWS], st.at[0], a_send.at[0], a_recv.at[0], ax=peer)

    def axial_down(peer):
        return remote(st.at[1], st.at[ROWS + 1], a_send.at[1], a_recv.at[1], ax=peer)

    sub = lax.broadcasted_iota(jnp.int32, TILE, 0)
    lane = lax.broadcasted_iota(jnp.int32, TILE, 1)

    pair = lax.div(lane, 2)

    def pack(i, carry):
        got = [zero] * 4
        for c in range(HV):
            k = c * 4 // HV
            got[k] = jnp.where(pair == c, roll(st[1 + i, c], 2 * c + 1, 1), got[k])
        ps[i] = (got[0] + got[1]) + (got[2] + got[3])
        return carry

    lax.fori_loop(0, ROWS, pack, 0)
    pitch_next = remote(ps, pr.at[0], p_send.at[0], p_recv.at[0], pit=pit_next)
    pitch_prev = remote(ps, pr.at[1], p_send.at[1], p_recv.at[1], pit=pit_prev)

    row = lax.rem(sub, 4)
    is_row = [row == j for j in range(4)]

    def packed_rows(rows):
        up = rows[3]
        down = rows[0]
        for j in range(3):
            up = jnp.where(is_row[j], roll(rows[j], j - 3, 0), up)
        for j in range(1, 4):
            down = jnp.where(is_row[j], roll(rows[j], j, 0), down)
        return up, down

    def packed(g, c):
        return packed_rows([st[1 + 4 * g + j, c] for j in range(4)])

    def speed_of(x):
        return 1.0 + 0.5 * jnp.tanh(x)

    def tables(i, carry):
        s = speed_of(st[1 + i, 0])
        spd[1 + i] = s
        coef = coef_of(i)
        radius = s * limit + (6.0 * dissipation + HARM // 2 * blade_freq)
        fac[i] = (-0.5 * section_weight * courant) * jnp.sqrt(1.0 + 4.0 * coef) / (coef * radius)
        return carry

    lax.fori_loop(0, ROWS, tables, 0)

    for t in range(2):
        for g in range(4):
            up, down = packed_rows([fac[4 * g + j] * wl[t, 4 * g + j] for j in range(4)])
            wsend[0, t, g] = down
            wsend[1, t, g] = up

    def weights(side, peer):
        return remote(wsend.at[side], wrecv.at[side], w_send.at[side], w_recv.at[side], rad=peer)

    swap_blocks = remote(fs, fx, g_send.at[0], g_recv.at[0], ax=partner)
    tell = remote(mo.at[0], mi.at[0], g_send.at[1], g_recv.at[1], ax=partner)

    def pass_pivot(peer):
        return remote(mo.at[1], mi.at[1], g_send.at[2], g_recv.at[2], ax=peer)

    lower = core == 0

    def through_block(block, x):
        a, b, c_prev, d_prev = (block[k] for k in range(4))
        low = jnp.where(lower, a + c_prev, c_prev + d_prev)
        high = jnp.where(lower, b + d_prev, a + b)
        return (jnp.where(lower, a, d_prev) * x + b) / (low * x + high)

    def serve_pivots():
        swap_blocks.wait_recv()

        @pl.when(gets)
        def _():
            pass_pivot(chain_from).wait_recv()

        inner = through_block(fs, mi[1])
        mo[0] = inner
        mo[1] = through_block(fx, inner)
        tell.start()

        @pl.when(passes)
        def _():
            pass_pivot(chain_to).start()

    def partial(side, peer):
        return remote(part_s.at[side], part_r.at[side], q_send.at[side], q_recv.at[side], rad=peer)

    radial_peers = jnp.minimum(rad, 1) + jnp.minimum(nrad - 1 - rad, 1)
    axial_peers = jnp.minimum(ax, 2) + jnp.minimum(nax - 1 - ax, 2)
    pl.semaphore_wait(barrier, 2 + axial_peers + radial_peers)
    swap_blocks.start()
    pitch_next.start()
    pitch_prev.start()

    @pl.when(ax < nax - 1)
    def _():
        axial_up(ax + 1).start()

    @pl.when(ax > 0)
    def _():
        axial_down(ax - 1).start()

    @pl.when(rad > 0)
    def _():
        weights(0, rad - 1).start()

    @pl.when(rad < nrad - 1)
    def _():
        weights(1, rad + 1).start()

    def radial_up(h, peer):
        return remote(rs.at[0, h], rr.at[0, h], r_send.at[0, h], r_recv.at[0, h], rad=peer)

    def radial_down(h, peer):
        return remote(rs.at[1, h], rr.at[1, h], r_send.at[1, h], r_recv.at[1, h], rad=peer)

    def send_radial(h, carry):
        @pl.when(rad < nrad - 1)
        def _():
            radial_up(h, rad + 1).start()

        @pl.when(rad > 0)
        def _():
            radial_down(h, rad - 1).start()

        return carry

    for g in range(4):
        up, down = packed(g, 0)
        spk[0, g] = speed_of(up)
        spk[1, g] = speed_of(down)

    def radial(h, carry):
        def group(g, carry):
            su, sd = spk[0, g], spk[1, g]
            ups, downs, wups, wdowns = [], [], [], []
            for v in range(VARS):
                up, down = packed(g, h * VARS + v)
                ups.append(up)
                downs.append(down)
                wups.append(su * up)
                wdowns.append(sd * down)
            for v in range(VARS):
                tu = -2.0 * dissipation * ups[v]
                td = -2.0 * dissipation * downs[v]
                for w in range(VARS):
                    m = am[49 + v * 7 + w]
                    tu = tu - m * wups[w]
                    td = td + m * wdowns[w]
                rs[0, h, g, v] = tu
                rs[1, h, g, v] = td
            return carry

        lax.fori_loop(0, 4, group, 0)

        @pl.when(h < 2)
        def _():
            send_radial(h, 0)

        return carry

    lax.fori_loop(0, HARM, radial, 0)

    @pl.when(far < 5)
    def _():
        serve_pivots()

    def weigh(side):
        def harmonic(h, carry):
            for pair_at in range(4):
                got = zero
                for m in range(4):
                    v = 2 * pair_at + m // 2
                    if v == VARS:
                        continue
                    x = zero
                    for g in range(4):
                        x = x + wrecv[side, m % 2, g] * rs[side, h, g, v]
                    turn = 1 if side else -1
                    x = x + roll(x, turn, 0)
                    x = x + roll(x, 2 * turn, 0)
                    target = 3 - m if side else m
                    got = jnp.where(is_row[target], roll(x, -turn * m, 0), got)
                part_s[side, h, pair_at] = got
            return carry

        lax.fori_loop(0, HARM, harmonic, 0)

    def return_sums():
        @pl.when(rad < nrad - 1)
        def _():
            weights(0, rad + 1).wait_recv()
            weigh(0)
            partial(0, rad + 1).start()

        @pl.when(rad > 0)
        def _():
            weights(1, rad - 1).wait_recv()
            weigh(1)
            partial(1, rad - 1).start()

        lax.fori_loop(2, HARM, send_radial, 0)

    first_lane = lane == 0
    last_lane = lane == 127
    inner_low = row > 0
    inner_high = row < 3

    def straight(i):
        sa, sc, sb = spd[i], spd[1 + i], spd[2 + i]
        su = roll(sc, 1, 0)
        sd = roll(sc, -1, 0)
        for h in range(HARM):
            d0, d1, acc = [], [], []
            for v in range(VARS):
                c = h * VARS + v
                here, back, ahead = st[1 + i, c], st[i, c], st[2 + i, c]
                under = jnp.where(inner_low, roll(here, 1, 0), 0.0)
                over = jnp.where(inner_high, roll(here, -1, 0), 0.0)
                d0.append(sb * ahead - sa * back)
                d1.append(sd * over - su * under)
                around = (back + ahead) + (under + over)
                acc.append(12.0 * dissipation * here - 2.0 * dissipation * around)
                if h:
                    k = (h + 1) // 2
                    twin = st[1 + i, c + VARS if h % 2 else c - VARS]
                    sign = 2.0 * k * blade_freq if h % 2 else -2.0 * k * blade_freq
                    acc[v] = acc[v] + sign * twin
            for v in range(VARS):
                t = acc[v]
                for w in range(VARS):
                    t = t + am[v * 7 + w] * d0[w]
                    t = t + am[49 + v * 7 + w] * d1[w]
                bb[i, h * VARS + v] = t

    def inner_rows(step, carry):
        @pl.when(step == 6)
        def _():
            return_sums()

        straight(step + 1)
        return carry

    lax.fori_loop(0, ROWS - 2, inner_rows, 0)

    @pl.when(ax > 0)
    def _():
        axial_up(ax - 1).wait_recv()

    @pl.when(ax < nax - 1)
    def _():
        axial_down(ax + 1).wait_recv()

    spd[0] = speed_of(st[0, 0])
    spd[ROWS + 1] = speed_of(st[ROWS + 1, 0])

    def outer_rows(step, carry):
        straight((ROWS - 1) * step)
        return carry

    lax.fori_loop(0, 2, outer_rows, 0)

    @pl.when(far == 5)
    def _():
        serve_pivots()

    pitch_next.wait_recv()
    pitch_prev.wait_recv()
    top = sub >= 4
    even = lax.rem(lane, 2) == 0

    def merge(i, carry):
        own = ps[i]
        before = jnp.where(top, pr[0, i], own)
        after = jnp.where(top, own, pr[1, i])
        both = jnp.where(even, roll(after, -1, 1), roll(before, 1, 1))
        pe[i] = roll(both, 4, 0)
        return carry

    lax.fori_loop(0, ROWS, merge, 0)

    def sideways(i, carry):
        pitched = pe[i]
        scale = fac[i]
        sl = sr = None
        for h in range(HARM):
            d2, acc = [], []
            for v in range(VARS):
                c = h * VARS + v
                here = st[1 + i, c]
                e = roll(pitched, -(2 * c + 1), 1)
                left = jnp.where(first_lane, e, roll(here, 1, 1))
                right = jnp.where(last_lane, e, roll(here, -1, 1))
                if c == 0:
                    sl, sr = speed_of(left), speed_of(right)
                d2.append(sr * right - sl * left)
                acc.append(bb[i, c] - 2.0 * dissipation * (left + right))
            for v in range(VARS):
                t = acc[v]
                for w in range(VARS):
                    t = t + am[98 + v * 7 + w] * d2[w]
                bb[i, h * VARS + v] = scale * t
        return carry

    lax.fori_loop(0, ROWS, sideways, 0)

    @pl.when(far > 5)
    def _():
        serve_pivots()

    tell.wait_recv()
    e_in = jnp.where(lower, mi[1], mi[0])
    f_in = jnp.where(lower, mi[0], mi[1])

    n, m = e_in, one
    for i in range(ROWS):
        n = n + dlt[i] * m
        after = n + m
        inv = 1.0 / after
        qq[i] = m * inv
        ww[i] = inv
        m = after
    e_out = n * inv
    n, m = f_in, one
    for i in reversed(range(ROWS)):
        n = n + dlt[i] * m
        m = n + m
    inv = 1.0 / m
    ends[0] = ww[ROWS - 1]
    ends[1] = inv
    ends[2] = 1.0 - f_in
    ends[3] = 1.0 / (e_out + f_in * qq[ROWS - 1])
    send_ends = remote(ends.at[pl.ds(0, 2)], part_ends, e_send, e_recv, ax=partner)
    send_ends.start()

    edge_low = is_row[0]
    edge_high = is_row[3]
    def piece(h):
        return pl.ds(h * VARS, VARS)

    def swap(h):
        return remote(
            x1s.at[1 - core, piece(h)], x1r.at[piece(h)], s_send.at[h], s_recv.at[h], ax=partner
        )

    @pl.when(rad > 0)
    def _():
        partial(0, rad - 1).wait_recv()

    @pl.when(rad < nrad - 1)
    def _():
        partial(1, rad + 1).wait_recv()

    q_in, s_in = 1.0 - e_in, 1.0 - f_in
    mix_first = wl[1, ROWS - 1] * q_in / (e_in + f_own * q_in)
    mix_last = wl[0, 0] * s_in / (f_in + e_own * s_in)

    def block_ends(h, carry):
        def group(g, sums):
            sums = list(sums)
            for j in range(4):
                i = 4 * g + j
                last, first = wl[0, i], wl[1, i]
                for v in range(VARS):
                    right = bb[i, h * VARS + v]
                    sums[2 * v] = sums[2 * v] + last * right
                    sums[2 * v + 1] = sums[2 * v + 1] + first * right
            return tuple(sums)

        sums = list(lax.fori_loop(0, 4, group, (zero,) * (2 * VARS)))
        for at in range(2 * VARS):
            m = at % 4
            low = roll(part_r[0, h, at // 4], -m, 0)
            high = roll(part_r[1, h, at // 4], m, 0)
            sums[at] = sums[at] + jnp.where(edge_low, low, jnp.where(edge_high, high, 0.0))
        for v in range(VARS):
            x1s[0, h * VARS + v] = sums[2 * v] + mix_first * sums[2 * v + 1]
            x1s[1, h * VARS + v] = sums[2 * v + 1] + mix_last * sums[2 * v]
        swap(h).start()
        return carry

    lax.fori_loop(0, HARM, block_ends, 0)

    def eliminate(h, carry):
        @pl.when(rad > 0)
        def _():
            radial_up(h, rad - 1).wait_recv()

        @pl.when(rad < nrad - 1)
        def _():
            radial_down(h, rad + 1).wait_recv()

        def group(g, carry):
            carried = list(carry)
            for j in range(4):
                i = 4 * g + j
                scale, q = fac[i], qq[i]
                for v in range(VARS):
                    low = roll(rr[0, h, g, v], -j, 0)
                    high = roll(rr[1, h, g, v], 3 - j, 0)
                    extra = jnp.where(edge_low, low, jnp.where(edge_high, high, 0.0))
                    right = bb[i, h * VARS + v] + scale * extra
                    carried[v] = q * (right + carried[v])
                    bb[i, h * VARS + v] = carried[v]
            return tuple(carried)

        lax.fori_loop(0, 4, group, (zero,) * VARS)
        return carry

    def chain(h, peer):
        return remote(cout.at[piece(h)], cin.at[piece(h)], c_send.at[h], c_recv.at[h], ax=peer)

    def back(h):
        return remote(x2s.at[piece(h)], x2r.at[piece(h)], b_send.at[h], b_recv.at[h], ax=partner)

    send_ends.wait_recv()

    def relay(h, carry):
        swap(h).wait_recv()

        @pl.when(gets)
        def _():
            chain(h, chain_from).wait_recv()

        own_factor = ends[core]
        other_factor = part_ends[core]
        through = own_factor * other_factor
        for v in range(VARS):
            c = h * VARS + v
            x, own = cin[c], x1s[core, c]
            cout[c] = through * x + (other_factor * own + x1r[c])
            x2s[c] = own_factor * x + own

        @pl.when(passes)
        def _():
            chain(h, chain_to).start()

        back(h).start()
        return carry

    relay_turn = lax.div(far, 5)

    def turn(t, carry):
        @pl.when(t == relay_turn)
        def _():
            lax.fori_loop(0, HARM, relay, 0)

        @pl.when(t == 0)
        def _():
            lax.fori_loop(0, HARM, eliminate, 0)

        return carry

    lax.fori_loop(0, 2, turn, 0)

    def finish_copy(h):
        part = pl.ds(h * VARS, VARS)
        return pltpu.make_async_copy(bb.at[:, part], out_hbm.at[:, part], out_sem.at[h])

    def finish(h, carry):
        back(h).wait_recv()
        entering, after = [], []
        for v in range(VARS):
            c = h * VARS + v
            held, given = cin[c], x2r[c]
            p = jnp.where(lower, held, given)
            r = jnp.where(lower, given, held)
            whole = ends[0] * p + x1s[0, c]
            entering.append(p)
            after.append((r + ends[2] * whole) * ends[3])

        def back_row(t, after):
            i = ROWS - 1 - t
            q, w = qq[i], ww[i]
            following = []
            for v in range(VARS):
                c = h * VARS + v
                x = (bb[i, c] + w * entering[v]) + q * after[v]
                following.append(x)
                bb[i, c] = st[1 + i, c] + x
            return tuple(following)

        lax.fori_loop(0, ROWS, back_row, tuple(after))
        finish_copy(h).start()
        return carry

    lax.fori_loop(0, HARM, finish, 0)

    @pl.when(ax < nax - 1)
    def _():
        axial_up(ax + 1).wait_send()

    @pl.when(ax > 0)
    def _():
        axial_down(ax - 1).wait_send()

    swap_blocks.wait_send()
    tell.wait_send()

    @pl.when(passes)
    def _():
        pass_pivot(chain_to).wait_send()

    pitch_next.wait_send()
    pitch_prev.wait_send()
    send_ends.wait_send()

    @pl.when(rad > 0)
    def _():
        weights(0, rad - 1).wait_send()
        partial(1, rad - 1).wait_send()

    @pl.when(rad < nrad - 1)
    def _():
        weights(1, rad + 1).wait_send()
        partial(0, rad + 1).wait_send()

    def sent_pieces(h, carry):
        @pl.when(rad < nrad - 1)
        def _():
            radial_up(h, rad + 1).wait_send()

        @pl.when(rad > 0)
        def _():
            radial_down(h, rad - 1).wait_send()

        @pl.when(passes)
        def _():
            chain(h, chain_to).wait_send()

        swap(h).wait_send()
        back(h).wait_send()
        return carry

    lax.fori_loop(0, HARM, sent_pieces, 0)

    def written(h, carry):
        finish_copy(h).wait()
        return carry

    lax.fori_loop(0, HARM, written, 0)


def solution(mesh):
    sizes = (mesh.shape["ax"], mesh.shape["rad"], mesh.shape["pit"])
    nax = sizes[0]

    def to_tiles(x):
        lead = x.shape[:-2]
        x = x.reshape(lead + (4, 2, 128))
        n = len(lead)
        x = x.transpose(tuple(range(n)) + (n + 1, n, n + 2))
        return x.reshape(lead + TILE)

    def from_tiles(x):
        lead = x.shape[:-2]
        x = x.reshape(lead + (2, 4, 128))
        n = len(lead)
        x = x.transpose(tuple(range(n)) + (n + 1, n, n + 2))
        return x.reshape(lead + (4, 256))

    def vmem(*lead):
        return pltpu.VMEM(lead + TILE, F32)

    dma = pltpu.SemaphoreType.DMA

    def on_device(state, flux_jac, line_coef, line_mask):
        out = pl.pallas_call(
            functools.partial(kernel, sizes),
            out_shape=jax.ShapeDtypeStruct((ROWS, HV) + TILE, F32),
            in_specs=[
                pl.BlockSpec(memory_space=pltpu.HBM),
                pl.BlockSpec(memory_space=pltpu.HBM),
                pl.BlockSpec(memory_space=pltpu.HBM),
                pl.BlockSpec(memory_space=pltpu.HBM),
            ],
            out_specs=pl.BlockSpec(memory_space=pl.ANY),
            scratch_shapes=[
                pltpu.SMEM((3, VARS, VARS), F32),
                vmem(),
                pltpu.VMEM((ROWS,) + TILE, jnp.int32),
                vmem(ROWS + 2, HV),
                vmem(ROWS, HV),
                vmem(2, HARM, 4, VARS),
                vmem(2, HARM, 4, VARS),
                vmem(ROWS),
                vmem(2, ROWS),
                vmem(ROWS),
                vmem(4),
                vmem(4),
                vmem(2),
                vmem(2),
                vmem(3 * VARS * VARS),
                vmem(ROWS),
                vmem(ROWS),
                vmem(ROWS),
                vmem(ROWS),
                vmem(ROWS + 2),
                vmem(2, 4),
                vmem(4),
                vmem(2),
                vmem(2, HV),
                vmem(HV),
                vmem(HV),
                vmem(HV),
                vmem(HV),
                vmem(HV),
                vmem(2, ROWS),
                vmem(2, 2, 4),
                vmem(2, 2, 4),
                vmem(2, HARM, 4),
                vmem(2, HARM, 4),
                dma((4,)),
                dma((HARM,)),
                dma((2,)),
                dma((2,)),
                dma((2, HARM)),
                dma((2, HARM)),
                dma((2,)),
                dma((2,)),
                dma((3,)),
                dma((3,)),
                dma,
                dma,
                dma((HARM,)),
                dma((HARM,)),
                dma((HARM,)),
                dma((HARM,)),
                dma((HARM,)),
                dma((HARM,)),
                dma((2,)),
                dma((2,)),
                dma((2,)),
                dma((2,)),
            ],
            compiler_params=pltpu.CompilerParams(
                collective_id=0, has_side_effects=True, vmem_limit_bytes=40 * 1024 * 1024
            ),
        )(*(pltpu.with_memory_space_constraint(x, pltpu.HBM) for x in (to_tiles(state), flux_jac, to_tiles(line_coef), to_tiles(line_mask))))
        return from_tiles(out)

    return jax.shard_map(
        on_device,
        mesh=mesh,
        in_specs=(P("ax", None, "rad", "pit"), P(), P("rad", "pit"), P("ax", "rad", "pit")),
        out_specs=P("ax", None, "rad", "pit"),
        check_vma=False,
    )
```

```python
import functools

import jax
import jax.numpy as jnp
from jax import lax
from jax.experimental import pallas as pl
from jax.experimental.pallas import tpu as pltpu
from jax.sharding import PartitionSpec as P

HARM = 7
VARS = 7
HV = HARM * VARS
ROWS = 16
PIECE = 3
PIECES = -(-HV // PIECE)
PAD = PIECE * PIECES
MESH = pl.DeviceIdType.MESH

blade_freq = 0.6
dissipation = 0.2
courant = 1.0
section_weight = 0.5

F32 = jnp.float32
TILE = (8, 128)


def remote(src, dst, send, recv, **place):
    return pltpu.make_async_remote_copy(
        src_ref=src, dst_ref=dst, send_sem=send, recv_sem=recv, device_id=place, device_id_type=MESH
    )


def roll(x, shift, axis):
    shift = shift % x.shape[axis]
    return pltpu.roll(x, shift, axis) if shift else x


def kernel(
    sizes,
    state_hbm,
    jac_hbm,
    line_hbm,
    mask_hbm,
    out_hbm,
    jac,
    line,
    mask,
    st,
    bb,
    rs,
    rr,
    ps,
    pr,
    pe,
    fs,
    fx,
    mo,
    mi,
    am,
    dlt,
    qq,
    ww,
    fac,
    spd,
    spk,
    ends,
    products,
    x1s,
    xt,
    x1r,
    cin,
    cout,
    x2s,
    x2r,
    wl,
    wsend,
    wrecv,
    part_s,
    part_r,
    in_sem,
    out_sem,
    a_send,
    a_recv,
    r_send,
    r_recv,
    p_send,
    p_recv,
    g_send,
    g_recv,
    s_send,
    s_recv,
    b_send,
    b_recv,
    c_send,
    c_recv,
    w_send,
    w_recv,
    q_send,
    q_recv,
):
    nax, nrad, npit = sizes
    chips = nax // 2
    ax = lax.axis_index("ax")
    rad = lax.axis_index("rad")
    pit = lax.axis_index("pit")
    core = lax.rem(ax, 2)
    chip = lax.div(ax, 2)
    partner = ax + 1 - 2 * core
    pit_next = lax.rem(pit + 1, npit)
    pit_prev = lax.rem(pit + npit - 1, npit)
    zero = jnp.zeros(TILE, F32)
    one = jnp.ones(TILE, F32)

    load = pltpu.make_async_copy(state_hbm, st.at[pl.ds(1, ROWS)], in_sem.at[0])
    load.start()
    load_jac = pltpu.make_async_copy(jac_hbm, jac, in_sem.at[1])
    load_jac.start()
    load_line = pltpu.make_async_copy(line_hbm, line, in_sem.at[2])
    load_line.start()
    load_mask = pltpu.make_async_copy(mask_hbm, mask, in_sem.at[3])
    load_mask.start()

    barrier = pltpu.get_barrier_semaphore()

    for offset in (-2, -1, 1, 2):

        @pl.when((ax + offset >= 0) & (ax + offset < nax))
        def _():
            pl.semaphore_signal(
                barrier, inc=1, device_id={"ax": ax + offset}, device_id_type=MESH
            )

    pl.semaphore_signal(barrier, inc=1, device_id={"pit": pit_next}, device_id_type=MESH)
    pl.semaphore_signal(barrier, inc=1, device_id={"pit": pit_prev}, device_id_type=MESH)

    @pl.when(rad > 0)
    def _():
        pl.semaphore_signal(barrier, inc=1, device_id={"rad": rad - 1}, device_id_type=MESH)

    @pl.when(rad < nrad - 1)
    def _():
        pl.semaphore_signal(barrier, inc=1, device_id={"rad": rad + 1}, device_id_type=MESH)

    load_jac.wait()
    for d in range(3):
        for v in range(VARS):
            for w in range(VARS):
                am[d * 49 + v * 7 + w] = jnp.full(TILE, jac[d, v, w], F32)
    limit = zero
    for d in range(3):
        largest = zero
        for v in range(VARS):
            total = zero
            for w in range(VARS):
                total = total + jnp.abs(am[d * 49 + v * 7 + w])
            largest = jnp.maximum(largest, total)
        limit = limit + largest

    load_line.wait()
    load_mask.wait()
    base = line[...]

    def coef_of(i):
        return base * (1.0 + mask[i].astype(F32))

    a, b, c, d_, c_prev, d_prev = one, zero, zero, one, zero, one
    heads = []
    for i in range(ROWS):
        inv = 1.0 / coef_of(i)
        dlt[i] = inv
        heads.append(c + d_)
        c_prev, d_prev = c, d_
        a = a + inv * c
        b = b + inv * d_
        c = a + c
        d_ = b + d_
    inv = 1.0 / (c + d_)
    for i in range(ROWS):
        wl[0, i] = heads[i] * inv
    e_own = (a + b) * inv
    n, m = one, one
    heads = []
    for i in reversed(range(ROWS)):
        heads.append((i, m))
        n = n + dlt[i] * m
        m = n + m
    inv = 1.0 / m
    for i, value in heads:
        wl[1, i] = value * inv
    f_own = n * inv
    fs[0] = a
    fs[1] = b
    fs[2] = c_prev
    fs[3] = d_prev

    for side, edge in ((0, 0), (1, nrad - 1)):

        @pl.when(rad == edge)
        def _():
            def clear(h, carry):
                for g in range(4):
                    for v in range(VARS):
                        rr[side, h, g, v] = zero
                    part_r[side, h, g] = zero
                return carry

            lax.fori_loop(0, HARM, clear, 0)

    @pl.when(ax == 0)
    def _():
        def clear(c, carry):
            st[0, c] = zero
            return carry

        lax.fori_loop(0, HV, clear, 0)

    @pl.when(ax == nax - 1)
    def _():
        def clear(c, carry):
            st[ROWS + 1, c] = zero
            return carry

        lax.fori_loop(0, HV, clear, 0)

    far = jnp.where(core == 0, chip, chips - 1 - chip)
    passes = far < chips - 1
    gets = far > 0
    chain_to = ax + 2 - 4 * core
    chain_from = ax - 2 + 4 * core

    @pl.when(far == 0)
    def _():
        mi[1] = one
        for c in range(PAD):
            cin[c] = zero

    load.wait()

    def axial_up(peer):
        return remote(st.at[ROWS], st.at[0], a_send.at[0], a_recv.at[0], ax=peer)

    def axial_down(peer):
        return remote(st.at[1], st.at[ROWS + 1], a_send.at[1], a_recv.at[1], ax=peer)

    sub = lax.broadcasted_iota(jnp.int32, TILE, 0)
    lane = lax.broadcasted_iota(jnp.int32, TILE, 1)

    pair = lax.div(lane, 2)

    def pack(i, carry):
        got = [zero] * 4
        for c in range(HV):
            k = c * 4 // HV
            got[k] = jnp.where(pair == c, roll(st[1 + i, c], 2 * c + 1, 1), got[k])
        ps[i] = (got[0] + got[1]) + (got[2] + got[3])
        return carry

    lax.fori_loop(0, ROWS, pack, 0)
    pitch_next = remote(ps, pr.at[0], p_send.at[0], p_recv.at[0], pit=pit_next)
    pitch_prev = remote(ps, pr.at[1], p_send.at[1], p_recv.at[1], pit=pit_prev)

    row = lax.rem(sub, 4)
    is_row = [row == j for j in range(4)]

    def packed_rows(rows):
        up = rows[3]
        down = rows[0]
        for j in range(3):
            up = jnp.where(is_row[j], roll(rows[j], j - 3, 0), up)
        for j in range(1, 4):
            down = jnp.where(is_row[j], roll(rows[j], j, 0), down)
        return up, down

    def packed(g, c):
        return packed_rows([st[1 + 4 * g + j, c] for j in range(4)])

    def speed_of(x):
        return 1.0 + 0.5 * jnp.tanh(x)

    def tables(i, carry):
        s = speed_of(st[1 + i, 0])
        spd[1 + i] = s
        coef = coef_of(i)
        radius = s * limit + (6.0 * dissipation + HARM // 2 * blade_freq)
        fac[i] = (-0.5 * section_weight * courant) * jnp.sqrt(1.0 + 4.0 * coef) / (coef * radius)
        return carry

    lax.fori_loop(0, ROWS, tables, 0)

    for t in range(2):
        for g in range(4):
            up, down = packed_rows([fac[4 * g + j] * wl[t, 4 * g + j] for j in range(4)])
            wsend[0, t, g] = down
            wsend[1, t, g] = up

    def weights(side, peer):
        return remote(wsend.at[side], wrecv.at[side], w_send.at[side], w_recv.at[side], rad=peer)

    swap_blocks = remote(fs, fx, g_send.at[0], g_recv.at[0], ax=partner)
    tell = remote(mo.at[0], mi.at[0], g_send.at[1], g_recv.at[1], ax=partner)

    def pass_pivot(peer):
        return remote(mo.at[1], mi.at[1], g_send.at[2], g_recv.at[2], ax=peer)

    lower = core == 0

    def through_block(block, x):
        a, b, c_prev, d_prev = (block[k] for k in range(4))
        low = jnp.where(lower, a + c_prev, c_prev + d_prev)
        high = jnp.where(lower, b + d_prev, a + b)
        inv = 1.0 / (low * x + high)
        return (jnp.where(lower, a, d_prev) * x + b) * inv, inv

    def serve_pivots():
        swap_blocks.wait_recv()

        @pl.when(gets)
        def _():
            pass_pivot(chain_from).wait_recv()

        inner, own = through_block(fs, mi[1])
        outer, other = through_block(fx, inner)
        mo[0] = inner
        mo[1] = outer
        products[0] = own
        products[1] = other
        tell.start()

        @pl.when(passes)
        def _():
            pass_pivot(chain_to).start()

    def partial(side, peer):
        return remote(part_s.at[side], part_r.at[side], q_send.at[side], q_recv.at[side], rad=peer)

    radial_peers = jnp.minimum(rad, 1) + jnp.minimum(nrad - 1 - rad, 1)
    axial_peers = jnp.minimum(ax, 2) + jnp.minimum(nax - 1 - ax, 2)
    pl.semaphore_wait(barrier, 2 + axial_peers + radial_peers)
    swap_blocks.start()
    pitch_next.start()
    pitch_prev.start()

    @pl.when(ax < nax - 1)
    def _():
        axial_up(ax + 1).start()

    @pl.when(ax > 0)
    def _():
        axial_down(ax - 1).start()

    @pl.when(rad > 0)
    def _():
        weights(0, rad - 1).start()

    @pl.when(rad < nrad - 1)
    def _():
        weights(1, rad + 1).start()

    def radial_up(h, peer):
        return remote(rs.at[0, h], rr.at[0, h], r_send.at[0, h], r_recv.at[0, h], rad=peer)

    def radial_down(h, peer):
        return remote(rs.at[1, h], rr.at[1, h], r_send.at[1, h], r_recv.at[1, h], rad=peer)

    def send_radial(h, carry):
        @pl.when(rad < nrad - 1)
        def _():
            radial_up(h, rad + 1).start()

        @pl.when(rad > 0)
        def _():
            radial_down(h, rad - 1).start()

        return carry

    for g in range(4):
        up, down = packed(g, 0)
        spk[0, g] = speed_of(up)
        spk[1, g] = speed_of(down)

    def radial(h, carry):
        def group(g, carry):
            su, sd = spk[0, g], spk[1, g]
            ups, downs, wups, wdowns = [], [], [], []
            for v in range(VARS):
                up, down = packed(g, h * VARS + v)
                ups.append(up)
                downs.append(down)
                wups.append(su * up)
                wdowns.append(sd * down)
            for v in range(VARS):
                tu = -2.0 * dissipation * ups[v]
                td = -2.0 * dissipation * downs[v]
                for w in range(VARS):
                    m = am[49 + v * 7 + w]
                    tu = tu - m * wups[w]
                    td = td + m * wdowns[w]
                rs[0, h, g, v] = tu
                rs[1, h, g, v] = td
            return carry

        lax.fori_loop(0, 4, group, 0)

        @pl.when(h < 2)
        def _():
            send_radial(h, 0)

        return carry

    lax.fori_loop(0, HARM, radial, 0)

    @pl.when(far < 2)
    def _():
        serve_pivots()

    def weigh(side):
        def harmonic(h, carry):
            for pair_at in range(4):
                got = zero
                for m in range(4):
                    v = 2 * pair_at + m // 2
                    if v == VARS:
                        continue
                    x = zero
                    for g in range(4):
                        x = x + wrecv[side, m % 2, g] * rs[side, h, g, v]
                    turn = 1 if side else -1
                    x = x + roll(x, turn, 0)
                    x = x + roll(x, 2 * turn, 0)
                    target = 3 - m if side else m
                    got = jnp.where(is_row[target], roll(x, -turn * m, 0), got)
                part_s[side, h, pair_at] = got
            return carry

        lax.fori_loop(0, HARM, harmonic, 0)

    def return_sums():
        @pl.when(rad < nrad - 1)
        def _():
            weights(0, rad + 1).wait_recv()
            weigh(0)
            partial(0, rad + 1).start()

        @pl.when(rad > 0)
        def _():
            weights(1, rad - 1).wait_recv()
            weigh(1)
            partial(1, rad - 1).start()

        lax.fori_loop(2, HARM, send_radial, 0)

    first_lane = lane == 0
    last_lane = lane == 127
    inner_low = row > 0
    inner_high = row < 3

    def straight(i):
        sa, sc, sb = spd[i], spd[1 + i], spd[2 + i]
        su = roll(sc, 1, 0)
        sd = roll(sc, -1, 0)
        for h in range(HARM):
            d0, d1, acc = [], [], []
            for v in range(VARS):
                c = h * VARS + v
                here, back, ahead = st[1 + i, c], st[i, c], st[2 + i, c]
                under = jnp.where(inner_low, roll(here, 1, 0), 0.0)
                over = jnp.where(inner_high, roll(here, -1, 0), 0.0)
                d0.append(sb * ahead - sa * back)
                d1.append(sd * over - su * under)
                around = (back + ahead) + (under + over)
                acc.append(12.0 * dissipation * here - 2.0 * dissipation * around)
                if h:
                    k = (h + 1) // 2
                    twin = st[1 + i, c + VARS if h % 2 else c - VARS]
                    sign = 2.0 * k * blade_freq if h % 2 else -2.0 * k * blade_freq
                    acc[v] = acc[v] + sign * twin
            for v in range(VARS):
                t = acc[v]
                for w in range(VARS):
                    t = t + am[v * 7 + w] * d0[w]
                    t = t + am[49 + v * 7 + w] * d1[w]
                bb[i, h * VARS + v] = t

    def inner_rows(step, carry):
        @pl.when(step == 6)
        def _():
            return_sums()

        straight(step + 1)
        return carry

    lax.fori_loop(0, ROWS - 2, inner_rows, 0)

    @pl.when(ax > 0)
    def _():
        axial_up(ax - 1).wait_recv()

    @pl.when(ax < nax - 1)
    def _():
        axial_down(ax + 1).wait_recv()

    spd[0] = speed_of(st[0, 0])
    spd[ROWS + 1] = speed_of(st[ROWS + 1, 0])

    def outer_rows(step, carry):
        straight((ROWS - 1) * step)
        return carry

    lax.fori_loop(0, 2, outer_rows, 0)

    @pl.when((far >= 2) & (far < 4))
    def _():
        serve_pivots()

    pitch_next.wait_recv()
    pitch_prev.wait_recv()
    top = sub >= 4
    even = lax.rem(lane, 2) == 0

    def merge(i, carry):
        own = ps[i]
        before = jnp.where(top, pr[0, i], own)
        after = jnp.where(top, own, pr[1, i])
        both = jnp.where(even, roll(after, -1, 1), roll(before, 1, 1))
        pe[i] = roll(both, 4, 0)
        return carry

    lax.fori_loop(0, ROWS, merge, 0)

    def sideways(i, carry):
        pitched = pe[i]
        scale = fac[i]
        sl = sr = None
        for h in range(HARM):
            d2, acc = [], []
            for v in range(VARS):
                c = h * VARS + v
                here = st[1 + i, c]
                e = roll(pitched, -(2 * c + 1), 1)
                left = jnp.where(first_lane, e, roll(here, 1, 1))
                right = jnp.where(last_lane, e, roll(here, -1, 1))
                if c == 0:
                    sl, sr = speed_of(left), speed_of(right)
                d2.append(sr * right - sl * left)
                acc.append(bb[i, c] - 2.0 * dissipation * (left + right))
            for v in range(VARS):
                t = acc[v]
                for w in range(VARS):
                    t = t + am[98 + v * 7 + w] * d2[w]
                bb[i, h * VARS + v] = scale * t
        return carry

    lax.fori_loop(0, ROWS, sideways, 0)

    edge_low = is_row[0]
    edge_high = is_row[3]
    def piece(k):
        return pl.ds(k * PIECE, PIECE)

    def swap(k):
        return remote(
            xt.at[1 - core, piece(k)], x1r.at[piece(k)], s_send.at[k], s_recv.at[k], ax=partner
        )

    def chain(k, peer):
        return remote(cout.at[piece(k)], cin.at[piece(k)], c_send.at[k], c_recv.at[k], ax=peer)

    def back(k):
        return remote(x2s.at[piece(k)], x2r.at[piece(k)], b_send.at[k], b_recv.at[k], ax=partner)

    @pl.when(rad > 0)
    def _():
        partial(0, rad - 1).wait_recv()

    @pl.when(rad < nrad - 1)
    def _():
        partial(1, rad + 1).wait_recv()

    def block_ends(h, carry):
        def group(g, sums):
            sums = list(sums)
            for j in range(4):
                i = 4 * g + j
                last, first = wl[0, i], wl[1, i]
                for v in range(VARS):
                    right = bb[i, h * VARS + v]
                    sums[2 * v] = sums[2 * v] + last * right
                    sums[2 * v + 1] = sums[2 * v + 1] + first * right
            return tuple(sums)

        sums = list(lax.fori_loop(0, 4, group, (zero,) * (2 * VARS)))
        for at in range(2 * VARS):
            m = at % 4
            low = roll(part_r[0, h, at // 4], -m, 0)
            high = roll(part_r[1, h, at // 4], m, 0)
            sums[at] = sums[at] + jnp.where(edge_low, low, jnp.where(edge_high, high, 0.0))
        for v in range(VARS):
            x1s[0, h * VARS + v] = sums[2 * v]
            x1s[1, h * VARS + v] = sums[2 * v + 1]
        return carry

    lax.fori_loop(0, HARM, block_ends, 0)
    for t in range(2):
        for c in range(HV, PAD):
            x1s[t, c] = zero

    def share(x, edge):
        rest = 1.0 - x
        return wl[0, 0] * rest / (x + edge * rest)

    def eliminate(h, carry):
        @pl.when(rad > 0)
        def _():
            radial_up(h, rad - 1).wait_recv()

        @pl.when(rad < nrad - 1)
        def _():
            radial_down(h, rad + 1).wait_recv()

        def group(g, carry):
            carried = list(carry)
            for j in range(4):
                i = 4 * g + j
                scale, q = fac[i], qq[i]
                for v in range(VARS):
                    low = roll(rr[0, h, g, v], -j, 0)
                    high = roll(rr[1, h, g, v], 3 - j, 0)
                    extra = jnp.where(edge_low, low, jnp.where(edge_high, high, 0.0))
                    right = bb[i, h * VARS + v] + scale * extra
                    carried[v] = q * (right + carried[v])
                    bb[i, h * VARS + v] = carried[v]
            return tuple(carried)

        lax.fori_loop(0, 4, group, (zero,) * VARS)
        return carry

    def give():
        tell.wait_recv()
        part = share(mi[0], jnp.where(lower, e_own, f_own))

        def one_piece(k, carry):
            for m in range(PIECE):
                c = k * PIECE + m
                xt[1 - core, c] = x1s[1 - core, c] + part * x1s[core, c]
            swap(k).start()
            return carry

        lax.fori_loop(0, PIECES, one_piece, 0)

    def relay_all():
        part = share(mi[1], jnp.where(lower, f_own, e_own))
        own_factor = products[0]
        other_factor = products[1]
        through = own_factor * other_factor

        def one_piece(k, carry):
            swap(k).wait_recv()
            owns, offers = [], []
            for m in range(PIECE):
                c = k * PIECE + m
                own = x1s[core, c] + part * x1s[1 - core, c]
                xt[core, c] = own
                owns.append(own)
                offers.append(other_factor * own + x1r[c])

            @pl.when(gets)
            def _():
                chain(k, chain_from).wait_recv()

            for m in range(PIECE):
                c = k * PIECE + m
                x = cin[c]
                cout[c] = through * x + offers[m]
                x2s[c] = own_factor * x + owns[m]

            @pl.when(passes)
            def _():
                chain(k, chain_to).start()

            back(k).start()
            return carry

        lax.fori_loop(0, PIECES, one_piece, 0)

    @pl.when(far >= 4)
    def _():
        give()
        serve_pivots()

    @pl.when(far < chips - 1)
    def _():
        relay_all()

    @pl.when(far < 4)
    def _():
        give()

    e_in = jnp.where(lower, mi[1], mi[0])
    f_in = jnp.where(lower, mi[0], mi[1])
    n, m = e_in, one
    for i in range(ROWS):
        n = n + dlt[i] * m
        after = n + m
        inv = 1.0 / after
        qq[i] = m * inv
        ww[i] = inv
        m = after
    e_out = n * inv
    ends[0] = inv
    ends[1] = 1.0 - f_in
    ends[2] = 1.0 / (e_out + f_in * qq[ROWS - 1])

    lax.fori_loop(0, HARM, eliminate, 0)

    @pl.when(far == chips - 1)
    def _():
        relay_all()

    def finish_copy(h):
        part = pl.ds(h * VARS, VARS)
        return pltpu.make_async_copy(bb.at[:, part], out_hbm.at[:, part], out_sem.at[h])

    def finish(h, carry):
        def returned(k, carry):
            back(k).wait_recv()
            return carry

        first = lax.div(h * VARS + PIECE - 1, PIECE)
        last = lax.div((h + 1) * VARS + PIECE - 1, PIECE)
        lax.fori_loop(first, last, returned, 0)
        entering, after = [], []
        for v in range(VARS):
            c = h * VARS + v
            held, given = cin[c], x2r[c]
            p = jnp.where(lower, held, given)
            r = jnp.where(lower, given, held)
            whole = ends[0] * p + xt[0, c]
            entering.append(p)
            after.append((r + ends[1] * whole) * ends[2])

        def back_row(t, after):
            i = ROWS - 1 - t
            q, w = qq[i], ww[i]
            following = []
            for v in range(VARS):
                c = h * VARS + v
                x = (bb[i, c] + w * entering[v]) + q * after[v]
                following.append(x)
                bb[i, c] = st[1 + i, c] + x
            return tuple(following)

        lax.fori_loop(0, ROWS, back_row, tuple(after))
        finish_copy(h).start()
        return carry

    lax.fori_loop(0, HARM, finish, 0)

    @pl.when(ax < nax - 1)
    def _():
        axial_up(ax + 1).wait_send()

    @pl.when(ax > 0)
    def _():
        axial_down(ax - 1).wait_send()

    swap_blocks.wait_send()
    tell.wait_send()

    @pl.when(passes)
    def _():
        pass_pivot(chain_to).wait_send()

    pitch_next.wait_send()
    pitch_prev.wait_send()

    @pl.when(rad > 0)
    def _():
        weights(0, rad - 1).wait_send()
        partial(1, rad - 1).wait_send()

    @pl.when(rad < nrad - 1)
    def _():
        weights(1, rad + 1).wait_send()
        partial(0, rad + 1).wait_send()

    def sent_pieces(h, carry):
        @pl.when(rad < nrad - 1)
        def _():
            radial_up(h, rad + 1).wait_send()

        @pl.when(rad > 0)
        def _():
            radial_down(h, rad - 1).wait_send()

        return carry

    lax.fori_loop(0, HARM, sent_pieces, 0)

    def sent_chain(k, carry):
        @pl.when(passes)
        def _():
            chain(k, chain_to).wait_send()

        swap(k).wait_send()
        back(k).wait_send()
        return carry

    lax.fori_loop(0, PIECES, sent_chain, 0)

    def written(h, carry):
        finish_copy(h).wait()
        return carry

    lax.fori_loop(0, HARM, written, 0)


def solution(mesh):
    sizes = (mesh.shape["ax"], mesh.shape["rad"], mesh.shape["pit"])
    nax = sizes[0]

    def to_tiles(x):
        lead = x.shape[:-2]
        x = x.reshape(lead + (4, 2, 128))
        n = len(lead)
        x = x.transpose(tuple(range(n)) + (n + 1, n, n + 2))
        return x.reshape(lead + TILE)

    def from_tiles(x):
        lead = x.shape[:-2]
        x = x.reshape(lead + (2, 4, 128))
        n = len(lead)
        x = x.transpose(tuple(range(n)) + (n + 1, n, n + 2))
        return x.reshape(lead + (4, 256))

    def vmem(*lead):
        return pltpu.VMEM(lead + TILE, F32)

    dma = pltpu.SemaphoreType.DMA

    def on_device(state, flux_jac, line_coef, line_mask):
        out = pl.pallas_call(
            functools.partial(kernel, sizes),
            out_shape=jax.ShapeDtypeStruct((ROWS, HV) + TILE, F32),
            in_specs=[
                pl.BlockSpec(memory_space=pltpu.HBM),
                pl.BlockSpec(memory_space=pltpu.HBM),
                pl.BlockSpec(memory_space=pltpu.HBM),
                pl.BlockSpec(memory_space=pltpu.HBM),
            ],
            out_specs=pl.BlockSpec(memory_space=pl.ANY),
            scratch_shapes=[
                pltpu.SMEM((3, VARS, VARS), F32),
                vmem(),
                pltpu.VMEM((ROWS,) + TILE, jnp.int32),
                vmem(ROWS + 2, HV),
                vmem(ROWS, HV),
                vmem(2, HARM, 4, VARS),
                vmem(2, HARM, 4, VARS),
                vmem(ROWS),
                vmem(2, ROWS),
                vmem(ROWS),
                vmem(4),
                vmem(4),
                vmem(2),
                vmem(2),
                vmem(3 * VARS * VARS),
                vmem(ROWS),
                vmem(ROWS),
                vmem(ROWS),
                vmem(ROWS),
                vmem(ROWS + 2),
                vmem(2, 4),
                vmem(3),
                vmem(2),
                vmem(2, PAD),
                vmem(2, PAD),
                vmem(PAD),
                vmem(PAD),
                vmem(PAD),
                vmem(PAD),
                vmem(PAD),
                vmem(2, ROWS),
                vmem(2, 2, 4),
                vmem(2, 2, 4),
                vmem(2, HARM, 4),
                vmem(2, HARM, 4),
                dma((4,)),
                dma((HARM,)),
                dma((2,)),
                dma((2,)),
                dma((2, HARM)),
                dma((2, HARM)),
                dma((2,)),
                dma((2,)),
                dma((3,)),
                dma((3,)),
                dma((PIECES,)),
                dma((PIECES,)),
                dma((PIECES,)),
                dma((PIECES,)),
                dma((PIECES,)),
                dma((PIECES,)),
                dma((2,)),
                dma((2,)),
                dma((2,)),
                dma((2,)),
            ],
            compiler_params=pltpu.CompilerParams(
                collective_id=0, has_side_effects=True, vmem_limit_bytes=40 * 1024 * 1024
            ),
        )(*(pltpu.with_memory_space_constraint(x, pltpu.HBM) for x in (to_tiles(state), flux_jac, to_tiles(line_coef), to_tiles(line_mask))))
        return from_tiles(out)

    return jax.shard_map(
        on_device,
        mesh=mesh,
        in_specs=(P("ax", None, "rad", "pit"), P(), P("rad", "pit"), P("ax", "rad", "pit")),
        out_specs=P("ax", None, "rad", "pit"),
        check_vma=False,
    )
```

```python
import functools

import jax
import jax.numpy as jnp
from jax import lax
from jax.experimental import pallas as pl
from jax.experimental.pallas import tpu as pltpu
from jax.sharding import PartitionSpec as P

HARM = 7
VARS = 7
HV = HARM * VARS
ROWS = 16
PIECE = 3
PIECES = -(-HV // PIECE)
PAD = PIECE * PIECES
MESH = pl.DeviceIdType.MESH

blade_freq = 0.6
dissipation = 0.2
courant = 1.0
section_weight = 0.5

F32 = jnp.float32
TILE = (8, 128)


def remote(src, dst, send, recv, **place):
    return pltpu.make_async_remote_copy(
        src_ref=src, dst_ref=dst, send_sem=send, recv_sem=recv, device_id=place, device_id_type=MESH
    )


def roll(x, shift, axis):
    shift = shift % x.shape[axis]
    return pltpu.roll(x, shift, axis) if shift else x


def kernel(
    sizes,
    state_hbm,
    jac_hbm,
    line_hbm,
    mask_hbm,
    out,
    jac,
    line,
    mask,
    st,
    bb,
    rs,
    rr,
    ps,
    pr,
    pe,
    fs,
    fx,
    mo,
    mi,
    am,
    dlt,
    qq,
    ww,
    fac,
    spd,
    spk,
    ends,
    products,
    x1s,
    xt,
    x1r,
    cin,
    cout,
    x2s,
    x2r,
    wl,
    wsend,
    wrecv,
    part_s,
    part_r,
    in_sem,
    a_send,
    a_recv,
    r_send,
    r_recv,
    p_send,
    p_recv,
    g_send,
    g_recv,
    s_send,
    s_recv,
    b_send,
    b_recv,
    c_send,
    c_recv,
    w_send,
    w_recv,
    q_send,
    q_recv,
):
    nax, nrad, npit = sizes
    chips = nax // 2
    ax = lax.axis_index("ax")
    rad = lax.axis_index("rad")
    pit = lax.axis_index("pit")
    core = lax.rem(ax, 2)
    chip = lax.div(ax, 2)
    partner = ax + 1 - 2 * core
    pit_next = lax.rem(pit + 1, npit)
    pit_prev = lax.rem(pit + npit - 1, npit)
    zero = jnp.zeros(TILE, F32)
    one = jnp.ones(TILE, F32)

    load = pltpu.make_async_copy(state_hbm, st.at[pl.ds(1, ROWS)], in_sem.at[0])
    load.start()
    load_jac = pltpu.make_async_copy(jac_hbm, jac, in_sem.at[1])
    load_jac.start()
    load_line = pltpu.make_async_copy(line_hbm, line, in_sem.at[2])
    load_line.start()
    load_mask = pltpu.make_async_copy(mask_hbm, mask, in_sem.at[3])
    load_mask.start()

    barrier = pltpu.get_barrier_semaphore()

    for offset in (-2, -1, 1, 2):

        @pl.when((ax + offset >= 0) & (ax + offset < nax))
        def _():
            pl.semaphore_signal(
                barrier, inc=1, device_id={"ax": ax + offset}, device_id_type=MESH
            )

    pl.semaphore_signal(barrier, inc=1, device_id={"pit": pit_next}, device_id_type=MESH)
    pl.semaphore_signal(barrier, inc=1, device_id={"pit": pit_prev}, device_id_type=MESH)

    @pl.when(rad > 0)
    def _():
        pl.semaphore_signal(barrier, inc=1, device_id={"rad": rad - 1}, device_id_type=MESH)

    @pl.when(rad < nrad - 1)
    def _():
        pl.semaphore_signal(barrier, inc=1, device_id={"rad": rad + 1}, device_id_type=MESH)

    load_jac.wait()
    for d in range(3):
        for v in range(VARS):
            for w in range(VARS):
                am[d * 49 + v * 7 + w] = jnp.full(TILE, jac[d, v, w], F32)
    limit = zero
    for d in range(3):
        largest = zero
        for v in range(VARS):
            total = zero
            for w in range(VARS):
                total = total + jnp.abs(am[d * 49 + v * 7 + w])
            largest = jnp.maximum(largest, total)
        limit = limit + largest

    load_line.wait()
    load_mask.wait()
    base = line[...]

    def coef_of(i):
        return base * (1.0 + mask[i].astype(F32))

    a, b, c, d_, c_prev, d_prev = one, zero, zero, one, zero, one
    heads = []
    for i in range(ROWS):
        inv = 1.0 / coef_of(i)
        dlt[i] = inv
        heads.append(c + d_)
        c_prev, d_prev = c, d_
        a = a + inv * c
        b = b + inv * d_
        c = a + c
        d_ = b + d_
    inv = 1.0 / (c + d_)
    for i in range(ROWS):
        wl[0, i] = heads[i] * inv
    e_own = (a + b) * inv
    n, m = one, one
    heads = []
    for i in reversed(range(ROWS)):
        heads.append((i, m))
        n = n + dlt[i] * m
        m = n + m
    inv = 1.0 / m
    for i, value in heads:
        wl[1, i] = value * inv
    f_own = n * inv
    fs[0] = a
    fs[1] = b
    fs[2] = c_prev
    fs[3] = d_prev

    for side, edge in ((0, 0), (1, nrad - 1)):

        @pl.when(rad == edge)
        def _():
            def clear(h, carry):
                for g in range(4):
                    for v in range(VARS):
                        rr[side, h, g, v] = zero
                    part_r[side, h, g] = zero
                return carry

            lax.fori_loop(0, HARM, clear, 0)

    @pl.when(ax == 0)
    def _():
        def clear(c, carry):
            st[0, c] = zero
            return carry

        lax.fori_loop(0, HV, clear, 0)

    @pl.when(ax == nax - 1)
    def _():
        def clear(c, carry):
            st[ROWS + 1, c] = zero
            return carry

        lax.fori_loop(0, HV, clear, 0)

    far = jnp.where(core == 0, chip, chips - 1 - chip)
    passes = far < chips - 1
    gets = far > 0
    chain_to = ax + 2 - 4 * core
    chain_from = ax - 2 + 4 * core

    @pl.when(far == 0)
    def _():
        mi[1] = one
        for c in range(PAD):
            cin[c] = zero

    load.wait()

    def axial_up(peer):
        return remote(st.at[ROWS], st.at[0], a_send.at[0], a_recv.at[0], ax=peer)

    def axial_down(peer):
        return remote(st.at[1], st.at[ROWS + 1], a_send.at[1], a_recv.at[1], ax=peer)

    sub = lax.broadcasted_iota(jnp.int32, TILE, 0)
    lane = lax.broadcasted_iota(jnp.int32, TILE, 1)

    pair = lax.div(lane, 2)

    def pack(i, carry):
        got = [zero] * 4
        for c in range(HV):
            k = c * 4 // HV
            got[k] = jnp.where(pair == c, roll(st[1 + i, c], 2 * c + 1, 1), got[k])
        ps[i] = (got[0] + got[1]) + (got[2] + got[3])
        return carry

    lax.fori_loop(0, ROWS, pack, 0)
    pitch_next = remote(ps, pr.at[0], p_send.at[0], p_recv.at[0], pit=pit_next)
    pitch_prev = remote(ps, pr.at[1], p_send.at[1], p_recv.at[1], pit=pit_prev)

    row = lax.rem(sub, 4)
    is_row = [row == j for j in range(4)]

    def packed_rows(rows):
        up = rows[3]
        down = rows[0]
        for j in range(3):
            up = jnp.where(is_row[j], roll(rows[j], j - 3, 0), up)
        for j in range(1, 4):
            down = jnp.where(is_row[j], roll(rows[j], j, 0), down)
        return up, down

    def packed(g, c):
        return packed_rows([st[1 + 4 * g + j, c] for j in range(4)])

    def speed_of(x):
        return 1.0 + 0.5 * jnp.tanh(x)

    def tables(i, carry):
        s = speed_of(st[1 + i, 0])
        spd[1 + i] = s
        coef = coef_of(i)
        radius = s * limit + (6.0 * dissipation + HARM // 2 * blade_freq)
        fac[i] = (-0.5 * section_weight * courant) * jnp.sqrt(1.0 + 4.0 * coef) / (coef * radius)
        return carry

    lax.fori_loop(0, ROWS, tables, 0)

    for t in range(2):
        for g in range(4):
            up, down = packed_rows([fac[4 * g + j] * wl[t, 4 * g + j] for j in range(4)])
            wsend[0, t, g] = down
            wsend[1, t, g] = up

    def weights(side, peer):
        return remote(wsend.at[side], wrecv.at[side], w_send.at[side], w_recv.at[side], rad=peer)

    swap_blocks = remote(fs, fx, g_send.at[0], g_recv.at[0], ax=partner)
    tell = remote(mo.at[0], mi.at[0], g_send.at[1], g_recv.at[1], ax=partner)

    def pass_pivot(peer):
        return remote(mo.at[1], mi.at[1], g_send.at[2], g_recv.at[2], ax=peer)

    lower = core == 0

    def through_block(block, x):
        a, b, c_prev, d_prev = (block[k] for k in range(4))
        low = jnp.where(lower, a + c_prev, c_prev + d_prev)
        high = jnp.where(lower, b + d_prev, a + b)
        inv = 1.0 / (low * x + high)
        return (jnp.where(lower, a, d_prev) * x + b) * inv, inv

    def serve_pivots():
        swap_blocks.wait_recv()

        @pl.when(gets)
        def _():
            pass_pivot(chain_from).wait_recv()

        inner, own = through_block(fs, mi[1])
        outer, other = through_block(fx, inner)
        mo[0] = inner
        mo[1] = outer
        products[0] = own
        products[1] = other
        tell.start()

        @pl.when(passes)
        def _():
            pass_pivot(chain_to).start()

    def partial(side, peer):
        return remote(part_s.at[side], part_r.at[side], q_send.at[side], q_recv.at[side], rad=peer)

    radial_peers = jnp.minimum(rad, 1) + jnp.minimum(nrad - 1 - rad, 1)
    axial_peers = jnp.minimum(ax, 2) + jnp.minimum(nax - 1 - ax, 2)
    pl.semaphore_wait(barrier, 2 + axial_peers + radial_peers)
    swap_blocks.start()
    pitch_next.start()
    pitch_prev.start()

    @pl.when(ax < nax - 1)
    def _():
        axial_up(ax + 1).start()

    @pl.when(ax > 0)
    def _():
        axial_down(ax - 1).start()

    @pl.when(rad > 0)
    def _():
        weights(0, rad - 1).start()

    @pl.when(rad < nrad - 1)
    def _():
        weights(1, rad + 1).start()

    def radial_up(h, peer):
        return remote(rs.at[0, h], rr.at[0, h], r_send.at[0, h], r_recv.at[0, h], rad=peer)

    def radial_down(h, peer):
        return remote(rs.at[1, h], rr.at[1, h], r_send.at[1, h], r_recv.at[1, h], rad=peer)

    def send_radial(h, carry):
        @pl.when(rad < nrad - 1)
        def _():
            radial_up(h, rad + 1).start()

        @pl.when(rad > 0)
        def _():
            radial_down(h, rad - 1).start()

        return carry

    for g in range(4):
        up, down = packed(g, 0)
        spk[0, g] = speed_of(up)
        spk[1, g] = speed_of(down)

    def radial(h, carry):
        def group(g, carry):
            su, sd = spk[0, g], spk[1, g]
            ups, downs, wups, wdowns = [], [], [], []
            for v in range(VARS):
                up, down = packed(g, h * VARS + v)
                ups.append(up)
                downs.append(down)
                wups.append(su * up)
                wdowns.append(sd * down)
            for v in range(VARS):
                tu = -2.0 * dissipation * ups[v]
                td = -2.0 * dissipation * downs[v]
                for w in range(VARS):
                    m = am[49 + v * 7 + w]
                    tu = tu - m * wups[w]
                    td = td + m * wdowns[w]
                rs[0, h, g, v] = tu
                rs[1, h, g, v] = td
            return carry

        lax.fori_loop(0, 4, group, 0)

        @pl.when(h < 2)
        def _():
            send_radial(h, 0)

        return carry

    lax.fori_loop(0, HARM, radial, 0)

    @pl.when(far < 2)
    def _():
        serve_pivots()

    def weigh(side):
        def harmonic(h, carry):
            for pair_at in range(4):
                got = zero
                for m in range(4):
                    v = 2 * pair_at + m // 2
                    if v == VARS:
                        continue
                    x = zero
                    for g in range(4):
                        x = x + wrecv[side, m % 2, g] * rs[side, h, g, v]
                    turn = 1 if side else -1
                    x = x + roll(x, turn, 0)
                    x = x + roll(x, 2 * turn, 0)
                    target = 3 - m if side else m
                    got = jnp.where(is_row[target], roll(x, -turn * m, 0), got)
                part_s[side, h, pair_at] = got
            return carry

        lax.fori_loop(0, HARM, harmonic, 0)

    def return_sums():
        @pl.when(rad < nrad - 1)
        def _():
            weights(0, rad + 1).wait_recv()
            weigh(0)
            partial(0, rad + 1).start()

        @pl.when(rad > 0)
        def _():
            weights(1, rad - 1).wait_recv()
            weigh(1)
            partial(1, rad - 1).start()

        lax.fori_loop(2, HARM, send_radial, 0)

    first_lane = lane == 0
    last_lane = lane == 127
    inner_low = row > 0
    inner_high = row < 3

    def straight(i):
        sa, sc, sb = spd[i], spd[1 + i], spd[2 + i]
        su = roll(sc, 1, 0)
        sd = roll(sc, -1, 0)
        for h in range(HARM):
            d0, d1, acc = [], [], []
            for v in range(VARS):
                c = h * VARS + v
                here, back, ahead = st[1 + i, c], st[i, c], st[2 + i, c]
                under = jnp.where(inner_low, roll(here, 1, 0), 0.0)
                over = jnp.where(inner_high, roll(here, -1, 0), 0.0)
                d0.append(sb * ahead - sa * back)
                d1.append(sd * over - su * under)
                around = (back + ahead) + (under + over)
                acc.append(12.0 * dissipation * here - 2.0 * dissipation * around)
                if h:
                    k = (h + 1) // 2
                    twin = st[1 + i, c + VARS if h % 2 else c - VARS]
                    sign = 2.0 * k * blade_freq if h % 2 else -2.0 * k * blade_freq
                    acc[v] = acc[v] + sign * twin
            for v in range(VARS):
                t = acc[v]
                for w in range(VARS):
                    t = t + am[v * 7 + w] * d0[w]
                    t = t + am[49 + v * 7 + w] * d1[w]
                bb[i, h * VARS + v] = t

    def inner_rows(step, carry):
        @pl.when(step == 6)
        def _():
            return_sums()

        straight(step + 1)
        return carry

    lax.fori_loop(0, ROWS - 2, inner_rows, 0)

    @pl.when(ax > 0)
    def _():
        axial_up(ax - 1).wait_recv()

    @pl.when(ax < nax - 1)
    def _():
        axial_down(ax + 1).wait_recv()

    spd[0] = speed_of(st[0, 0])
    spd[ROWS + 1] = speed_of(st[ROWS + 1, 0])

    def outer_rows(step, carry):
        straight((ROWS - 1) * step)
        return carry

    lax.fori_loop(0, 2, outer_rows, 0)

    @pl.when((far >= 2) & (far < 4))
    def _():
        serve_pivots()

    pitch_next.wait_recv()
    pitch_prev.wait_recv()
    top = sub >= 4
    even = lax.rem(lane, 2) == 0

    def merge(i, carry):
        own = ps[i]
        before = jnp.where(top, pr[0, i], own)
        after = jnp.where(top, own, pr[1, i])
        both = jnp.where(even, roll(after, -1, 1), roll(before, 1, 1))
        pe[i] = roll(both, 4, 0)
        return carry

    lax.fori_loop(0, ROWS, merge, 0)

    def sideways(i, carry):
        pitched = pe[i]
        scale = fac[i]
        sl = sr = None
        for h in range(HARM):
            d2, acc = [], []
            for v in range(VARS):
                c = h * VARS + v
                here = st[1 + i, c]
                e = roll(pitched, -(2 * c + 1), 1)
                left = jnp.where(first_lane, e, roll(here, 1, 1))
                right = jnp.where(last_lane, e, roll(here, -1, 1))
                if c == 0:
                    sl, sr = speed_of(left), speed_of(right)
                d2.append(sr * right - sl * left)
                acc.append(bb[i, c] - 2.0 * dissipation * (left + right))
            for v in range(VARS):
                t = acc[v]
                for w in range(VARS):
                    t = t + am[98 + v * 7 + w] * d2[w]
                bb[i, h * VARS + v] = scale * t
        return carry

    lax.fori_loop(0, ROWS, sideways, 0)

    edge_low = is_row[0]
    edge_high = is_row[3]
    def piece(k):
        return pl.ds(k * PIECE, PIECE)

    def swap(k):
        return remote(
            xt.at[1 - core, piece(k)], x1r.at[piece(k)], s_send.at[k], s_recv.at[k], ax=partner
        )

    def chain(k, peer):
        return remote(cout.at[piece(k)], cin.at[piece(k)], c_send.at[k], c_recv.at[k], ax=peer)

    def back(k):
        return remote(x2s.at[piece(k)], x2r.at[piece(k)], b_send.at[k], b_recv.at[k], ax=partner)

    @pl.when(rad > 0)
    def _():
        partial(0, rad - 1).wait_recv()

    @pl.when(rad < nrad - 1)
    def _():
        partial(1, rad + 1).wait_recv()

    def block_ends(h, carry):
        def group(g, sums):
            sums = list(sums)
            for j in range(4):
                i = 4 * g + j
                last, first = wl[0, i], wl[1, i]
                for v in range(VARS):
                    right = bb[i, h * VARS + v]
                    sums[2 * v] = sums[2 * v] + last * right
                    sums[2 * v + 1] = sums[2 * v + 1] + first * right
            return tuple(sums)

        sums = list(lax.fori_loop(0, 4, group, (zero,) * (2 * VARS)))
        for at in range(2 * VARS):
            m = at % 4
            low = roll(part_r[0, h, at // 4], -m, 0)
            high = roll(part_r[1, h, at // 4], m, 0)
            sums[at] = sums[at] + jnp.where(edge_low, low, jnp.where(edge_high, high, 0.0))
        for v in range(VARS):
            x1s[0, h * VARS + v] = sums[2 * v]
            x1s[1, h * VARS + v] = sums[2 * v + 1]
        return carry

    lax.fori_loop(0, HARM, block_ends, 0)
    for t in range(2):
        for c in range(HV, PAD):
            x1s[t, c] = zero

    def share(x, edge):
        rest = 1.0 - x
        return wl[0, 0] * rest / (x + edge * rest)

    def eliminate(h, carry):
        @pl.when(rad > 0)
        def _():
            radial_up(h, rad - 1).wait_recv()

        @pl.when(rad < nrad - 1)
        def _():
            radial_down(h, rad + 1).wait_recv()

        def group(g, carry):
            carried = list(carry)
            for j in range(4):
                i = 4 * g + j
                scale, q = fac[i], qq[i]
                for v in range(VARS):
                    low = roll(rr[0, h, g, v], -j, 0)
                    high = roll(rr[1, h, g, v], 3 - j, 0)
                    extra = jnp.where(edge_low, low, jnp.where(edge_high, high, 0.0))
                    right = bb[i, h * VARS + v] + scale * extra
                    carried[v] = q * (right + carried[v])
                    bb[i, h * VARS + v] = carried[v]
            return tuple(carried)

        lax.fori_loop(0, 4, group, (zero,) * VARS)
        return carry

    def give():
        tell.wait_recv()
        part = share(mi[0], jnp.where(lower, e_own, f_own))

        def one_piece(k, carry):
            for m in range(PIECE):
                c = k * PIECE + m
                xt[1 - core, c] = x1s[1 - core, c] + part * x1s[core, c]
            swap(k).start()
            return carry

        lax.fori_loop(0, PIECES, one_piece, 0)

    def relay_all():
        part = share(mi[1], jnp.where(lower, f_own, e_own))
        own_factor = products[0]
        other_factor = products[1]
        through = own_factor * other_factor

        def one_piece(k, carry):
            swap(k).wait_recv()
            owns, offers = [], []
            for m in range(PIECE):
                c = k * PIECE + m
                own = x1s[core, c] + part * x1s[1 - core, c]
                xt[core, c] = own
                owns.append(own)
                offers.append(other_factor * own + x1r[c])

            @pl.when(gets)
            def _():
                chain(k, chain_from).wait_recv()

            for m in range(PIECE):
                c = k * PIECE + m
                x = cin[c]
                cout[c] = through * x + offers[m]
                x2s[c] = own_factor * x + owns[m]

            @pl.when(passes)
            def _():
                chain(k, chain_to).start()

            back(k).start()
            return carry

        lax.fori_loop(0, PIECES, one_piece, 0)

    @pl.when(far >= 4)
    def _():
        give()
        serve_pivots()

    @pl.when(far < chips - 1)
    def _():
        relay_all()

    @pl.when(far < 4)
    def _():
        give()

    e_in = jnp.where(lower, mi[1], mi[0])
    f_in = jnp.where(lower, mi[0], mi[1])
    n, m = e_in, one
    for i in range(ROWS):
        n = n + dlt[i] * m
        after = n + m
        inv = 1.0 / after
        qq[i] = m * inv
        ww[i] = inv
        m = after
    e_out = n * inv
    ends[0] = inv
    ends[1] = 1.0 - f_in
    ends[2] = 1.0 / (e_out + f_in * qq[ROWS - 1])

    lax.fori_loop(0, HARM, eliminate, 0)

    @pl.when(far == chips - 1)
    def _():
        relay_all()

    def finish(h, carry):
        def returned(k, carry):
            back(k).wait_recv()
            return carry

        first = lax.div(h * VARS + PIECE - 1, PIECE)
        last = lax.div((h + 1) * VARS + PIECE - 1, PIECE)
        lax.fori_loop(first, last, returned, 0)
        entering, after = [], []
        for v in range(VARS):
            c = h * VARS + v
            held, given = cin[c], x2r[c]
            p = jnp.where(lower, held, given)
            r = jnp.where(lower, given, held)
            whole = ends[0] * p + xt[0, c]
            entering.append(p)
            after.append((r + ends[1] * whole) * ends[2])

        def back_row(t, after):
            i = ROWS - 1 - t
            q, w = qq[i], ww[i]
            following = []
            for v in range(VARS):
                c = h * VARS + v
                x = (bb[i, c] + w * entering[v]) + q * after[v]
                following.append(x)
                out[i, c] = st[1 + i, c] + x
            return tuple(following)

        lax.fori_loop(0, ROWS, back_row, tuple(after))
        return carry

    lax.fori_loop(0, HARM, finish, 0)

    @pl.when(ax < nax - 1)
    def _():
        axial_up(ax + 1).wait_send()

    @pl.when(ax > 0)
    def _():
        axial_down(ax - 1).wait_send()

    swap_blocks.wait_send()
    tell.wait_send()

    @pl.when(passes)
    def _():
        pass_pivot(chain_to).wait_send()

    pitch_next.wait_send()
    pitch_prev.wait_send()

    @pl.when(rad > 0)
    def _():
        weights(0, rad - 1).wait_send()
        partial(1, rad - 1).wait_send()

    @pl.when(rad < nrad - 1)
    def _():
        weights(1, rad + 1).wait_send()
        partial(0, rad + 1).wait_send()

    def sent_pieces(h, carry):
        @pl.when(rad < nrad - 1)
        def _():
            radial_up(h, rad + 1).wait_send()

        @pl.when(rad > 0)
        def _():
            radial_down(h, rad - 1).wait_send()

        return carry

    lax.fori_loop(0, HARM, sent_pieces, 0)

    def sent_chain(k, carry):
        @pl.when(passes)
        def _():
            chain(k, chain_to).wait_send()

        swap(k).wait_send()
        back(k).wait_send()
        return carry

    lax.fori_loop(0, PIECES, sent_chain, 0)


def solution(mesh):
    sizes = (mesh.shape["ax"], mesh.shape["rad"], mesh.shape["pit"])
    nax = sizes[0]

    def to_tiles(x):
        lead = x.shape[:-2]
        x = x.reshape(lead + (4, 2, 128))
        n = len(lead)
        x = x.transpose(tuple(range(n)) + (n + 1, n, n + 2))
        return x.reshape(lead + TILE)

    def from_tiles(x):
        lead = x.shape[:-2]
        x = x.reshape(lead + (2, 4, 128))
        n = len(lead)
        x = x.transpose(tuple(range(n)) + (n + 1, n, n + 2))
        return x.reshape(lead + (4, 256))

    def vmem(*lead):
        return pltpu.VMEM(lead + TILE, F32)

    dma = pltpu.SemaphoreType.DMA

    def on_device(state, flux_jac, line_coef, line_mask):
        out = pl.pallas_call(
            functools.partial(kernel, sizes),
            out_shape=jax.ShapeDtypeStruct((ROWS, HV) + TILE, F32),
            in_specs=[
                pl.BlockSpec(memory_space=pltpu.HBM),
                pl.BlockSpec(memory_space=pltpu.HBM),
                pl.BlockSpec(memory_space=pltpu.HBM),
                pl.BlockSpec(memory_space=pltpu.HBM),
            ],
            out_specs=pl.BlockSpec(memory_space=pltpu.VMEM),
            scratch_shapes=[
                pltpu.SMEM((3, VARS, VARS), F32),
                vmem(),
                pltpu.VMEM((ROWS,) + TILE, jnp.int32),
                vmem(ROWS + 2, HV),
                vmem(ROWS, HV),
                vmem(2, HARM, 4, VARS),
                vmem(2, HARM, 4, VARS),
                vmem(ROWS),
                vmem(2, ROWS),
                vmem(ROWS),
                vmem(4),
                vmem(4),
                vmem(2),
                vmem(2),
                vmem(3 * VARS * VARS),
                vmem(ROWS),
                vmem(ROWS),
                vmem(ROWS),
                vmem(ROWS),
                vmem(ROWS + 2),
                vmem(2, 4),
                vmem(3),
                vmem(2),
                vmem(2, PAD),
                vmem(2, PAD),
                vmem(PAD),
                vmem(PAD),
                vmem(PAD),
                vmem(PAD),
                vmem(PAD),
                vmem(2, ROWS),
                vmem(2, 2, 4),
                vmem(2, 2, 4),
                vmem(2, HARM, 4),
                vmem(2, HARM, 4),
                dma((4,)),
                dma((2,)),
                dma((2,)),
                dma((2, HARM)),
                dma((2, HARM)),
                dma((2,)),
                dma((2,)),
                dma((3,)),
                dma((3,)),
                dma((PIECES,)),
                dma((PIECES,)),
                dma((PIECES,)),
                dma((PIECES,)),
                dma((PIECES,)),
                dma((PIECES,)),
                dma((2,)),
                dma((2,)),
                dma((2,)),
                dma((2,)),
            ],
            compiler_params=pltpu.CompilerParams(
                collective_id=0, has_side_effects=True, vmem_limit_bytes=40 * 1024 * 1024
            ),
        )(*(pltpu.with_memory_space_constraint(x, pltpu.HBM) for x in (to_tiles(state), flux_jac, to_tiles(line_coef), to_tiles(line_mask))))
        return from_tiles(out)

    return jax.shard_map(
        on_device,
        mesh=mesh,
        in_specs=(P("ax", None, "rad", "pit"), P(), P("rad", "pit"), P("ax", "rad", "pit")),
        out_specs=P("ax", None, "rad", "pit"),
        check_vma=False,
    )
```

```python
import functools

import jax
import jax.numpy as jnp
from jax import lax
from jax.experimental import pallas as pl
from jax.experimental.pallas import tpu as pltpu
from jax.sharding import PartitionSpec as P

HARM = 7
VARS = 7
HV = HARM * VARS
ROWS = 16
PIECE = 3
PIECES = -(-HV // PIECE)
PAD = PIECE * PIECES
MESH = pl.DeviceIdType.MESH

blade_freq = 0.6
dissipation = 0.2
courant = 1.0
section_weight = 0.5

F32 = jnp.float32
TILE = (8, 128)


def remote(src, dst, send, recv, **place):
    return pltpu.make_async_remote_copy(
        src_ref=src, dst_ref=dst, send_sem=send, recv_sem=recv, device_id=place, device_id_type=MESH
    )


def roll(x, shift, axis):
    shift = shift % x.shape[axis]
    return pltpu.roll(x, shift, axis) if shift else x


def kernel(
    sizes,
    state_hbm,
    jac_hbm,
    line_hbm,
    mask_hbm,
    out,
    jac,
    line,
    mask,
    st,
    bb,
    rs,
    rr,
    ps,
    pr,
    pe,
    fs,
    fx,
    mo,
    mi,
    am,
    dlt,
    qq,
    ww,
    fac,
    spd,
    spk,
    ends,
    products,
    x1s,
    xt,
    x1r,
    cin,
    cout,
    x2s,
    x2r,
    wl,
    wsend,
    wrecv,
    part_s,
    part_r,
    in_sem,
    a_send,
    a_recv,
    r_send,
    r_recv,
    p_send,
    p_recv,
    g_send,
    g_recv,
    s_send,
    s_recv,
    b_send,
    b_recv,
    c_send,
    c_recv,
    w_send,
    w_recv,
    q_send,
    q_recv,
):
    nax, nrad, npit = sizes
    chips = nax // 2
    ax = lax.axis_index("ax")
    rad = lax.axis_index("rad")
    pit = lax.axis_index("pit")
    core = lax.rem(ax, 2)
    chip = lax.div(ax, 2)
    partner = ax + 1 - 2 * core
    pit_next = lax.rem(pit + 1, npit)
    pit_prev = lax.rem(pit + npit - 1, npit)
    zero = jnp.zeros(TILE, F32)
    one = jnp.ones(TILE, F32)

    load = pltpu.make_async_copy(state_hbm, st.at[pl.ds(1, ROWS)], in_sem.at[0])
    load.start()
    load_jac = pltpu.make_async_copy(jac_hbm, jac, in_sem.at[1])
    load_jac.start()
    load_line = pltpu.make_async_copy(line_hbm, line, in_sem.at[2])
    load_line.start()
    load_mask = pltpu.make_async_copy(mask_hbm, mask, in_sem.at[3])
    load_mask.start()

    barrier = pltpu.get_barrier_semaphore()

    for offset in (-2, -1, 1, 2):

        @pl.when((ax + offset >= 0) & (ax + offset < nax))
        def _():
            pl.semaphore_signal(
                barrier, inc=1, device_id={"ax": ax + offset}, device_id_type=MESH
            )

    pl.semaphore_signal(barrier, inc=1, device_id={"pit": pit_next}, device_id_type=MESH)
    pl.semaphore_signal(barrier, inc=1, device_id={"pit": pit_prev}, device_id_type=MESH)

    @pl.when(rad > 0)
    def _():
        pl.semaphore_signal(barrier, inc=1, device_id={"rad": rad - 1}, device_id_type=MESH)

    @pl.when(rad < nrad - 1)
    def _():
        pl.semaphore_signal(barrier, inc=1, device_id={"rad": rad + 1}, device_id_type=MESH)

    load_jac.wait()
    for d in range(3):
        for v in range(VARS):
            for w in range(VARS):
                am[d * 49 + v * 7 + w] = jnp.full(TILE, jac[d, v, w], F32)
    limit = zero
    for d in range(3):
        largest = zero
        for v in range(VARS):
            total = zero
            for w in range(VARS):
                total = total + jnp.abs(am[d * 49 + v * 7 + w])
            largest = jnp.maximum(largest, total)
        limit = limit + largest

    load_line.wait()
    load_mask.wait()
    base = line[...]

    def coef_of(i):
        return base * (1.0 + mask[i].astype(F32))

    a, b, c, d_, c_prev, d_prev = one, zero, zero, one, zero, one
    heads = []
    for i in range(ROWS):
        inv = 1.0 / coef_of(i)
        dlt[i] = inv
        heads.append(c + d_)
        c_prev, d_prev = c, d_
        a = a + inv * c
        b = b + inv * d_
        c = a + c
        d_ = b + d_
    inv = 1.0 / (c + d_)
    for i in range(ROWS):
        wl[0, i] = heads[i] * inv
    e_own = (a + b) * inv
    n, m = one, one
    heads = []
    for i in reversed(range(ROWS)):
        heads.append((i, m))
        n = n + dlt[i] * m
        m = n + m
    inv = 1.0 / m
    for i, value in heads:
        wl[1, i] = value * inv
    f_own = n * inv
    fs[0] = a
    fs[1] = b
    fs[2] = c_prev
    fs[3] = d_prev

    for side, edge in ((0, 0), (1, nrad - 1)):

        @pl.when(rad == edge)
        def _():
            def clear(h, carry):
                for g in range(4):
                    for v in range(VARS):
                        rr[side, h, g, v] = zero
                    part_r[side, h, g] = zero
                return carry

            lax.fori_loop(0, HARM, clear, 0)

    @pl.when(ax == 0)
    def _():
        def clear(c, carry):
            st[0, c] = zero
            return carry

        lax.fori_loop(0, HV, clear, 0)

    @pl.when(ax == nax - 1)
    def _():
        def clear(c, carry):
            st[ROWS + 1, c] = zero
            return carry

        lax.fori_loop(0, HV, clear, 0)

    far = jnp.where(core == 0, chip, chips - 1 - chip)
    passes = far < chips - 1
    gets = far > 0
    chain_to = ax + 2 - 4 * core
    chain_from = ax - 2 + 4 * core

    @pl.when(far == 0)
    def _():
        mi[1] = one
        for c in range(PAD):
            cin[c] = zero

    load.wait()

    def axial_up(peer):
        return remote(st.at[ROWS], st.at[0], a_send.at[0], a_recv.at[0], ax=peer)

    def axial_down(peer):
        return remote(st.at[1], st.at[ROWS + 1], a_send.at[1], a_recv.at[1], ax=peer)

    sub = lax.broadcasted_iota(jnp.int32, TILE, 0)
    lane = lax.broadcasted_iota(jnp.int32, TILE, 1)

    pair = lax.div(lane, 2)

    def pack(i, carry):
        got = [zero] * 4
        for c in range(HV):
            k = c * 4 // HV
            got[k] = jnp.where(pair == c, roll(st[1 + i, c], 2 * c + 1, 1), got[k])
        ps[i] = (got[0] + got[1]) + (got[2] + got[3])
        return carry

    lax.fori_loop(0, ROWS, pack, 0)
    pitch_next = remote(ps, pr.at[0], p_send.at[0], p_recv.at[0], pit=pit_next)
    pitch_prev = remote(ps, pr.at[1], p_send.at[1], p_recv.at[1], pit=pit_prev)

    row = lax.rem(sub, 4)
    is_row = [row == j for j in range(4)]

    def packed_rows(rows):
        up = rows[3]
        down = rows[0]
        for j in range(3):
            up = jnp.where(is_row[j], roll(rows[j], j - 3, 0), up)
        for j in range(1, 4):
            down = jnp.where(is_row[j], roll(rows[j], j, 0), down)
        return up, down

    def packed(g, c):
        return packed_rows([st[1 + 4 * g + j, c] for j in range(4)])

    def speed_of(x):
        return 1.0 + 0.5 * jnp.tanh(x)

    def tables(i, carry):
        s = speed_of(st[1 + i, 0])
        spd[1 + i] = s
        coef = coef_of(i)
        radius = s * limit + (6.0 * dissipation + HARM // 2 * blade_freq)
        fac[i] = (-0.5 * section_weight * courant) * jnp.sqrt(1.0 + 4.0 * coef) / (coef * radius)
        return carry

    lax.fori_loop(0, ROWS, tables, 0)

    for t in range(2):
        for g in range(4):
            up, down = packed_rows([fac[4 * g + j] * wl[t, 4 * g + j] for j in range(4)])
            wsend[0, t, g] = down
            wsend[1, t, g] = up

    def weights(side, peer):
        return remote(wsend.at[side], wrecv.at[side], w_send.at[side], w_recv.at[side], rad=peer)

    swap_blocks = remote(fs, fx, g_send.at[0], g_recv.at[0], ax=partner)
    tell = remote(mo.at[0], mi.at[0], g_send.at[1], g_recv.at[1], ax=partner)

    def pass_pivot(peer):
        return remote(mo.at[1], mi.at[1], g_send.at[2], g_recv.at[2], ax=peer)

    lower = core == 0

    def through_block(block, x):
        a, b, c_prev, d_prev = (block[k] for k in range(4))
        low = jnp.where(lower, a + c_prev, c_prev + d_prev)
        high = jnp.where(lower, b + d_prev, a + b)
        inv = 1.0 / (low * x + high)
        return (jnp.where(lower, a, d_prev) * x + b) * inv, inv

    def serve_pivots():
        swap_blocks.wait_recv()

        @pl.when(gets)
        def _():
            pass_pivot(chain_from).wait_recv()

        inner, own = through_block(fs, mi[1])
        outer, other = through_block(fx, inner)
        mo[0] = inner
        mo[1] = outer
        products[0] = own
        products[1] = other
        tell.start()

        @pl.when(passes)
        def _():
            pass_pivot(chain_to).start()

    def partial(side, peer):
        return remote(part_s.at[side], part_r.at[side], q_send.at[side], q_recv.at[side], rad=peer)

    radial_peers = jnp.minimum(rad, 1) + jnp.minimum(nrad - 1 - rad, 1)
    axial_peers = jnp.minimum(ax, 2) + jnp.minimum(nax - 1 - ax, 2)
    pl.semaphore_wait(barrier, 2 + axial_peers + radial_peers)
    swap_blocks.start()
    pitch_next.start()
    pitch_prev.start()

    @pl.when(ax < nax - 1)
    def _():
        axial_up(ax + 1).start()

    @pl.when(ax > 0)
    def _():
        axial_down(ax - 1).start()

    @pl.when(rad > 0)
    def _():
        weights(0, rad - 1).start()

    @pl.when(rad < nrad - 1)
    def _():
        weights(1, rad + 1).start()

    def radial_up(h, peer):
        return remote(rs.at[0, h], rr.at[0, h], r_send.at[0, h], r_recv.at[0, h], rad=peer)

    def radial_down(h, peer):
        return remote(rs.at[1, h], rr.at[1, h], r_send.at[1, h], r_recv.at[1, h], rad=peer)

    def send_radial(h, carry):
        @pl.when(rad < nrad - 1)
        def _():
            radial_up(h, rad + 1).start()

        @pl.when(rad > 0)
        def _():
            radial_down(h, rad - 1).start()

        return carry

    for g in range(4):
        up, down = packed(g, 0)
        spk[0, g] = speed_of(up)
        spk[1, g] = speed_of(down)

    def radial(h, carry):
        def group(g, carry):
            su, sd = spk[0, g], spk[1, g]
            ups, downs, wups, wdowns = [], [], [], []
            for v in range(VARS):
                up, down = packed(g, h * VARS + v)
                ups.append(up)
                downs.append(down)
                wups.append(su * up)
                wdowns.append(sd * down)
            for v in range(VARS):
                tu = -2.0 * dissipation * ups[v]
                td = -2.0 * dissipation * downs[v]
                for w in range(VARS):
                    m = am[49 + v * 7 + w]
                    tu = tu - m * wups[w]
                    td = td + m * wdowns[w]
                rs[0, h, g, v] = tu
                rs[1, h, g, v] = td
            return carry

        lax.fori_loop(0, 4, group, 0)

        @pl.when(h < 2)
        def _():
            send_radial(h, 0)

        return carry

    lax.fori_loop(0, HARM, radial, 0)

    @pl.when(far < 2)
    def _():
        serve_pivots()

    def weigh(side):
        def harmonic(h, carry):
            for pair_at in range(4):
                got = zero
                for m in range(4):
                    v = 2 * pair_at + m // 2
                    if v == VARS:
                        continue
                    x = zero
                    for g in range(4):
                        x = x + wrecv[side, m % 2, g] * rs[side, h, g, v]
                    turn = 1 if side else -1
                    x = x + roll(x, turn, 0)
                    x = x + roll(x, 2 * turn, 0)
                    target = 3 - m if side else m
                    got = jnp.where(is_row[target], roll(x, -turn * m, 0), got)
                part_s[side, h, pair_at] = got
            return carry

        lax.fori_loop(0, HARM, harmonic, 0)

    def return_sums():
        @pl.when(rad < nrad - 1)
        def _():
            weights(0, rad + 1).wait_recv()
            weigh(0)
            partial(0, rad + 1).start()

        @pl.when(rad > 0)
        def _():
            weights(1, rad - 1).wait_recv()
            weigh(1)
            partial(1, rad - 1).start()

        lax.fori_loop(2, HARM, send_radial, 0)

    first_lane = lane == 0
    last_lane = lane == 127
    inner_low = row > 0
    inner_high = row < 3

    def straight(i):
        sa, sc, sb = spd[i], spd[1 + i], spd[2 + i]
        su = roll(sc, 1, 0)
        sd = roll(sc, -1, 0)
        for h in range(HARM):
            d0, d1, acc = [], [], []
            for v in range(VARS):
                c = h * VARS + v
                here, back, ahead = st[1 + i, c], st[i, c], st[2 + i, c]
                under = jnp.where(inner_low, roll(here, 1, 0), 0.0)
                over = jnp.where(inner_high, roll(here, -1, 0), 0.0)
                d0.append(sb * ahead - sa * back)
                d1.append(sd * over - su * under)
                around = (back + ahead) + (under + over)
                acc.append(12.0 * dissipation * here - 2.0 * dissipation * around)
                if h:
                    k = (h + 1) // 2
                    twin = st[1 + i, c + VARS if h % 2 else c - VARS]
                    sign = 2.0 * k * blade_freq if h % 2 else -2.0 * k * blade_freq
                    acc[v] = acc[v] + sign * twin
            for v in range(VARS):
                t = acc[v]
                for w in range(VARS):
                    t = t + am[v * 7 + w] * d0[w]
                    t = t + am[49 + v * 7 + w] * d1[w]
                bb[i, h * VARS + v] = t

    def inner_rows(step, carry):
        @pl.when(step == 10)
        def _():
            return_sums()

        straight(step + 1)
        return carry

    lax.fori_loop(0, ROWS - 2, inner_rows, 0)

    @pl.when(ax > 0)
    def _():
        axial_up(ax - 1).wait_recv()

    @pl.when(ax < nax - 1)
    def _():
        axial_down(ax + 1).wait_recv()

    spd[0] = speed_of(st[0, 0])
    spd[ROWS + 1] = speed_of(st[ROWS + 1, 0])

    def outer_rows(step, carry):
        straight((ROWS - 1) * step)
        return carry

    lax.fori_loop(0, 2, outer_rows, 0)

    @pl.when((far >= 2) & (far < 4))
    def _():
        serve_pivots()

    pitch_next.wait_recv()
    pitch_prev.wait_recv()
    top = sub >= 4
    even = lax.rem(lane, 2) == 0

    def merge(i, carry):
        own = ps[i]
        before = jnp.where(top, pr[0, i], own)
        after = jnp.where(top, own, pr[1, i])
        both = jnp.where(even, roll(after, -1, 1), roll(before, 1, 1))
        pe[i] = roll(both, 4, 0)
        return carry

    lax.fori_loop(0, ROWS, merge, 0)

    def sideways(i, carry):
        pitched = pe[i]
        scale = fac[i]
        sl = sr = None
        for h in range(HARM):
            d2, acc = [], []
            for v in range(VARS):
                c = h * VARS + v
                here = st[1 + i, c]
                e = roll(pitched, -(2 * c + 1), 1)
                left = jnp.where(first_lane, e, roll(here, 1, 1))
                right = jnp.where(last_lane, e, roll(here, -1, 1))
                if c == 0:
                    sl, sr = speed_of(left), speed_of(right)
                d2.append(sr * right - sl * left)
                acc.append(bb[i, c] - 2.0 * dissipation * (left + right))
            for v in range(VARS):
                t = acc[v]
                for w in range(VARS):
                    t = t + am[98 + v * 7 + w] * d2[w]
                bb[i, h * VARS + v] = scale * t
        return carry

    lax.fori_loop(0, ROWS, sideways, 0)

    edge_low = is_row[0]
    edge_high = is_row[3]
    def piece(k):
        return pl.ds(k * PIECE, PIECE)

    def swap(k):
        return remote(
            xt.at[1 - core, piece(k)], x1r.at[piece(k)], s_send.at[k], s_recv.at[k], ax=partner
        )

    def chain(k, peer):
        return remote(cout.at[piece(k)], cin.at[piece(k)], c_send.at[k], c_recv.at[k], ax=peer)

    def back(k):
        return remote(x2s.at[piece(k)], x2r.at[piece(k)], b_send.at[k], b_recv.at[k], ax=partner)

    @pl.when(rad > 0)
    def _():
        partial(0, rad - 1).wait_recv()

    @pl.when(rad < nrad - 1)
    def _():
        partial(1, rad + 1).wait_recv()

    def block_ends(h, carry):
        def group(g, sums):
            sums = list(sums)
            for j in range(4):
                i = 4 * g + j
                last, first = wl[0, i], wl[1, i]
                for v in range(VARS):
                    right = bb[i, h * VARS + v]
                    sums[2 * v] = sums[2 * v] + last * right
                    sums[2 * v + 1] = sums[2 * v + 1] + first * right
            return tuple(sums)

        sums = list(lax.fori_loop(0, 4, group, (zero,) * (2 * VARS)))
        for at in range(2 * VARS):
            m = at % 4
            low = roll(part_r[0, h, at // 4], -m, 0)
            high = roll(part_r[1, h, at // 4], m, 0)
            sums[at] = sums[at] + jnp.where(edge_low, low, jnp.where(edge_high, high, 0.0))
        for v in range(VARS):
            x1s[0, h * VARS + v] = sums[2 * v]
            x1s[1, h * VARS + v] = sums[2 * v + 1]
        return carry

    lax.fori_loop(0, HARM, block_ends, 0)
    for t in range(2):
        for c in range(HV, PAD):
            x1s[t, c] = zero

    def share(x, edge):
        rest = 1.0 - x
        return wl[0, 0] * rest / (x + edge * rest)

    def eliminate(h, carry):
        @pl.when(rad > 0)
        def _():
            radial_up(h, rad - 1).wait_recv()

        @pl.when(rad < nrad - 1)
        def _():
            radial_down(h, rad + 1).wait_recv()

        def group(g, carry):
            carried = list(carry)
            for j in range(4):
                i = 4 * g + j
                scale, q = fac[i], qq[i]
                for v in range(VARS):
                    low = roll(rr[0, h, g, v], -j, 0)
                    high = roll(rr[1, h, g, v], 3 - j, 0)
                    extra = jnp.where(edge_low, low, jnp.where(edge_high, high, 0.0))
                    right = bb[i, h * VARS + v] + scale * extra
                    carried[v] = q * (right + carried[v])
                    bb[i, h * VARS + v] = carried[v]
            return tuple(carried)

        lax.fori_loop(0, 4, group, (zero,) * VARS)
        return carry

    def give():
        tell.wait_recv()
        part = share(mi[0], jnp.where(lower, e_own, f_own))

        def one_piece(k, carry):
            for m in range(PIECE):
                c = k * PIECE + m
                xt[1 - core, c] = x1s[1 - core, c] + part * x1s[core, c]
            swap(k).start()
            return carry

        lax.fori_loop(0, PIECES, one_piece, 0)

    def relay_all():
        part = share(mi[1], jnp.where(lower, f_own, e_own))
        own_factor = products[0]
        other_factor = products[1]
        through = own_factor * other_factor

        def one_piece(k, carry):
            swap(k).wait_recv()
            owns, offers = [], []
            for m in range(PIECE):
                c = k * PIECE + m
                own = x1s[core, c] + part * x1s[1 - core, c]
                xt[core, c] = own
                owns.append(own)
                offers.append(other_factor * own + x1r[c])

            @pl.when(gets)
            def _():
                chain(k, chain_from).wait_recv()

            for m in range(PIECE):
                c = k * PIECE + m
                x = cin[c]
                cout[c] = through * x + offers[m]
                x2s[c] = own_factor * x + owns[m]

            @pl.when(passes)
            def _():
                chain(k, chain_to).start()

            back(k).start()
            return carry

        lax.fori_loop(0, PIECES, one_piece, 0)

    @pl.when(far >= 4)
    def _():
        give()
        serve_pivots()

    @pl.when(far < chips - 1)
    def _():
        relay_all()

    @pl.when(far < 4)
    def _():
        give()

    e_in = jnp.where(lower, mi[1], mi[0])
    f_in = jnp.where(lower, mi[0], mi[1])
    n, m = e_in, one
    for i in range(ROWS):
        n = n + dlt[i] * m
        after = n + m
        inv = 1.0 / after
        qq[i] = m * inv
        ww[i] = inv
        m = after
    e_out = n * inv
    ends[0] = inv
    ends[1] = 1.0 - f_in
    ends[2] = 1.0 / (e_out + f_in * qq[ROWS - 1])

    lax.fori_loop(0, HARM, eliminate, 0)

    @pl.when(far == chips - 1)
    def _():
        relay_all()

    def finish(h, carry):
        def returned(k, carry):
            back(k).wait_recv()
            return carry

        first = lax.div(h * VARS + PIECE - 1, PIECE)
        last = lax.div((h + 1) * VARS + PIECE - 1, PIECE)
        lax.fori_loop(first, last, returned, 0)
        entering, after = [], []
        for v in range(VARS):
            c = h * VARS + v
            held, given = cin[c], x2r[c]
            p = jnp.where(lower, held, given)
            r = jnp.where(lower, given, held)
            whole = ends[0] * p + xt[0, c]
            entering.append(p)
            after.append((r + ends[1] * whole) * ends[2])

        def back_row(t, after):
            i = ROWS - 1 - t
            q, w = qq[i], ww[i]
            following = []
            for v in range(VARS):
                c = h * VARS + v
                x = (bb[i, c] + w * entering[v]) + q * after[v]
                following.append(x)
                out[i, c] = st[1 + i, c] + x
            return tuple(following)

        lax.fori_loop(0, ROWS, back_row, tuple(after))
        return carry

    lax.fori_loop(0, HARM, finish, 0)

    @pl.when(ax < nax - 1)
    def _():
        axial_up(ax + 1).wait_send()

    @pl.when(ax > 0)
    def _():
        axial_down(ax - 1).wait_send()

    swap_blocks.wait_send()
    tell.wait_send()

    @pl.when(passes)
    def _():
        pass_pivot(chain_to).wait_send()

    pitch_next.wait_send()
    pitch_prev.wait_send()

    @pl.when(rad > 0)
    def _():
        weights(0, rad - 1).wait_send()
        partial(1, rad - 1).wait_send()

    @pl.when(rad < nrad - 1)
    def _():
        weights(1, rad + 1).wait_send()
        partial(0, rad + 1).wait_send()

    def sent_pieces(h, carry):
        @pl.when(rad < nrad - 1)
        def _():
            radial_up(h, rad + 1).wait_send()

        @pl.when(rad > 0)
        def _():
            radial_down(h, rad - 1).wait_send()

        return carry

    lax.fori_loop(0, HARM, sent_pieces, 0)

    def sent_chain(k, carry):
        @pl.when(passes)
        def _():
            chain(k, chain_to).wait_send()

        swap(k).wait_send()
        back(k).wait_send()
        return carry

    lax.fori_loop(0, PIECES, sent_chain, 0)


def solution(mesh):
    sizes = (mesh.shape["ax"], mesh.shape["rad"], mesh.shape["pit"])
    nax = sizes[0]

    def to_tiles(x):
        lead = x.shape[:-2]
        x = x.reshape(lead + (4, 2, 128))
        n = len(lead)
        x = x.transpose(tuple(range(n)) + (n + 1, n, n + 2))
        return x.reshape(lead + TILE)

    def from_tiles(x):
        lead = x.shape[:-2]
        x = x.reshape(lead + (2, 4, 128))
        n = len(lead)
        x = x.transpose(tuple(range(n)) + (n + 1, n, n + 2))
        return x.reshape(lead + (4, 256))

    def vmem(*lead):
        return pltpu.VMEM(lead + TILE, F32)

    dma = pltpu.SemaphoreType.DMA

    def on_device(state, flux_jac, line_coef, line_mask):
        out = pl.pallas_call(
            functools.partial(kernel, sizes),
            out_shape=jax.ShapeDtypeStruct((ROWS, HV) + TILE, F32),
            in_specs=[
                pl.BlockSpec(memory_space=pltpu.HBM),
                pl.BlockSpec(memory_space=pltpu.HBM),
                pl.BlockSpec(memory_space=pltpu.HBM),
                pl.BlockSpec(memory_space=pltpu.HBM),
            ],
            out_specs=pl.BlockSpec(memory_space=pltpu.VMEM),
            scratch_shapes=[
                pltpu.SMEM((3, VARS, VARS), F32),
                vmem(),
                pltpu.VMEM((ROWS,) + TILE, jnp.int32),
                vmem(ROWS + 2, HV),
                vmem(ROWS, HV),
                vmem(2, HARM, 4, VARS),
                vmem(2, HARM, 4, VARS),
                vmem(ROWS),
                vmem(2, ROWS),
                vmem(ROWS),
                vmem(4),
                vmem(4),
                vmem(2),
                vmem(2),
                vmem(3 * VARS * VARS),
                vmem(ROWS),
                vmem(ROWS),
                vmem(ROWS),
                vmem(ROWS),
                vmem(ROWS + 2),
                vmem(2, 4),
                vmem(3),
                vmem(2),
                vmem(2, PAD),
                vmem(2, PAD),
                vmem(PAD),
                vmem(PAD),
                vmem(PAD),
                vmem(PAD),
                vmem(PAD),
                vmem(2, ROWS),
                vmem(2, 2, 4),
                vmem(2, 2, 4),
                vmem(2, HARM, 4),
                vmem(2, HARM, 4),
                dma((4,)),
                dma((2,)),
                dma((2,)),
                dma((2, HARM)),
                dma((2, HARM)),
                dma((2,)),
                dma((2,)),
                dma((3,)),
                dma((3,)),
                dma((PIECES,)),
                dma((PIECES,)),
                dma((PIECES,)),
                dma((PIECES,)),
                dma((PIECES,)),
                dma((PIECES,)),
                dma((2,)),
                dma((2,)),
                dma((2,)),
                dma((2,)),
            ],
            compiler_params=pltpu.CompilerParams(
                collective_id=0, has_side_effects=True, vmem_limit_bytes=40 * 1024 * 1024
            ),
        )(*(pltpu.with_memory_space_constraint(x, pltpu.HBM) for x in (to_tiles(state), flux_jac, to_tiles(line_coef), to_tiles(line_mask))))
        return from_tiles(out)

    return jax.shard_map(
        on_device,
        mesh=mesh,
        in_specs=(P("ax", None, "rad", "pit"), P(), P("rad", "pit"), P("ax", "rad", "pit")),
        out_specs=P("ax", None, "rad", "pit"),
        check_vma=False,
    )
```
